32 devices in a mesh: kx: 8 (over z, core), ky: 4 (over y, x).
Axes of the slice: x: 2, y: 2, z: 4, core: 2. Of those that a mesh axis runs over, the one named last changes fastest.
Arguments:
- kspace: bfloat16 [64, 16, 64, 256], P(None, 'kx', 'ky'), may hold values from -6 to 6
- kernel: bfloat16 [3, 3, 3, 64, 128], replicated, may hold values from -0.109375 to 0.109375
- mask: int32 [64, 256], P('ky'), may hold values 0 or 1
Outputs:
- updated: bfloat16 [64, 16, 64, 256], P(None, 'kx', 'ky')
- residual: bfloat16 [64, 16, 64, 256], P(None, 'kx', 'ky')
The draws below stay inside these ranges and needn't reach their ends.
All inputs are finite; a program needn't handle non-finite values. No bound on the sum of `mask` on one device may be relied on, other than what follows from the above.
Results may differ from the reference program's by a relative error of at most 0.0042.
Values may be sent and summed in bfloat16 or wider, within the bound.
No kernel may reach another device: no remote copies, remote signals or barrier semaphores. Data moves between devices by JAX's collectives and lax.ppermute only.
A program may use at most 128 MiB of HBM per device.

```python
import jax
import jax.numpy as jnp

CH = 64
NZ = 256
NX = 16
NY = 64


def with_ends(array, key, low, high):
    longest = array.shape.index(max(array.shape))
    spots = []
    for shift in (0, 1):
        where = [jax.random.randint(jax.random.fold_in(key, axis), (), 0, length) for axis, length in enumerate(array.shape)]
        where[longest] = (where[longest] + shift) % array.shape[longest]
        spots.append(tuple(where))
    return array.at[spots[0]].set(low).at[spots[1]].set(high)


def level_of(key, dims, shards, smallest, largest):
    def one(axis_at, shards_of):
        heights = jax.random.uniform(jax.random.fold_in(jax.random.fold_in(key, 6), axis_at), (shards_of,), jnp.float32, smallest / len(shards), largest / len(shards))
        return jnp.repeat(jnp.exp(heights), dims[axis_at] // shards_of).reshape((-1,) + (1,) * (len(dims) - axis_at - 1))

    gain = one(*shards[0])
    for cut in shards[1:]:
        gain = gain * one(*cut)
    return gain


def normal_values(stream_key, extent, spread, most, shards=(), dtype=jnp.bfloat16):
    values = spread * jax.random.normal(stream_key, extent, jnp.float32)
    if shards:
        values = values * level_of(stream_key, extent, shards, -0.22, 0.18)
    return jnp.clip(values, -most, most).astype(dtype)


def setup_inputs(seed: int = 0) -> dict:
    arg_keys = jax.random.split(jax.random.key(seed), 4)
    return {
        "kspace": normal_values(arg_keys[0], (CH, NX, NY, NZ), 1.0, 6.0, ((1, 8), (2, 4))),
        "kernel": normal_values(arg_keys[1], (3, 3, 3, CH, 2 * CH), (54 * CH) ** -0.5, 0.109375),
        "mask": with_ends((jax.random.randint(arg_keys[2], (NY, NZ), 0, 3) < 1).astype(jnp.int32), jax.random.fold_in(arg_keys[2], 1), 0, 1),
    }


step_size = 0.5


def channel_signs(count):
    half = count // 2
    return jnp.concatenate([jnp.ones((half,), jnp.float32), -jnp.ones((count - half,), jnp.float32)])


def forward_sum(extended, kernel):
    padded = jnp.pad(extended.astype(jnp.float32), ((0, 0), (1, 1), (1, 1), (1, 1)))
    total = jnp.zeros((CH, NX, NY, NZ), jnp.float32)
    for first in range(3):
        for second in range(3):
            for third in range(3):
                window = padded[:, first:first + NX, second:second + NY, third:third + NZ]
                weights = kernel[first, second, third].astype(jnp.float32)
                total = total + jnp.einsum("oi,ixyz->oxyz", weights, window)
    return total


def adjoint_sum(residual, kernel):
    padded = jnp.pad(residual.astype(jnp.float32), ((0, 0), (1, 1), (1, 1), (1, 1)))
    total = jnp.zeros((2 * CH, NX, NY, NZ), jnp.float32)
    for first in range(3):
        for second in range(3):
            for third in range(3):
                window = padded[:, 2 - first:2 - first + NX, 2 - second:2 - second + NY, 2 - third:2 - third + NZ]
                weights = kernel[first, second, third].astype(jnp.float32)
                total = total + jnp.einsum("oi,oxyz->ixyz", weights, window)
    return total


def reference(kspace, kernel, mask):
    signs = channel_signs(CH)[:, None, None, None]
    virtual = (signs * kspace[:, ::-1, ::-1, ::-1].astype(jnp.float32)).astype(jnp.bfloat16)
    extended = jnp.concatenate([kspace, virtual], axis=0)
    residual = (forward_sum(extended, kernel) - kspace.astype(jnp.float32)).astype(jnp.bfloat16)
    adjoint = adjoint_sum(residual, kernel)
    back = adjoint[CH:].astype(jnp.bfloat16)
    gradient = adjoint[:CH] - residual.astype(jnp.float32) + signs * back[:, ::-1, ::-1, ::-1].astype(jnp.float32)
    keep = 1.0 - mask.astype(jnp.float32)
    updated = (kspace.astype(jnp.float32) - step_size * keep[None, None] * gradient).astype(jnp.bfloat16)
    return updated, residual
```

```python
import jax
import jax.numpy as jnp
from jax import lax
from jax.experimental import pallas as pl
from jax.experimental.pallas import tpu as pltpu
from jax.sharding import PartitionSpec as P


step_size = 0.5
LANES = 128
AXES = ("kx", "ky")
f32 = jnp.float32
bf16 = jnp.bfloat16


def on_line(a, b, nx, ny):
    inner = min(a, nx - 1 - a)
    return inner if b < ny // 2 else nx - 1 - inner


def line_device(a, b, nx, ny, place):
    near = b if b < ny // 2 else ny - 1 - b
    inner = min(place, nx - 1 - place)
    return (inner if a < nx // 2 else nx - 1 - inner), (near if place < nx // 2 else ny - 1 - near)


def to_mirror(a, b, nx, ny):
    return nx - 1 - a, ny - 1 - b


def to_right(a, b, nx, ny):
    place = on_line(a, b, nx, ny) + 1
    return line_device(a, b, nx, ny, place) if place < nx else None


def to_left(a, b, nx, ny):
    place = on_line(a, b, nx, ny) - 1
    return line_device(a, b, nx, ny, place) if place >= 0 else None


def to_next(a, b, nx, ny):
    return (a, b + 1) if b + 1 < ny else None


def to_previous(a, b, nx, ny):
    return (a, b - 1) if b > 0 else None


def send(value, move):
    nx, ny = lax.axis_size("kx"), lax.axis_size("ky")
    pairs = []
    for a in range(nx):
        for b in range(ny):
            target = move(a, b, nx, ny)
            if target is not None:
                pairs.append((a * ny + b, target[0] * ny + target[1]))
    return lax.ppermute(value, AXES, pairs)


def place_flags():
    a, b = lax.axis_index("kx"), lax.axis_index("ky")
    nx, ny = lax.axis_size("kx"), lax.axis_size("ky")
    near = b < ny // 2
    direct = near == (a < nx // 2)
    fold = (a == nx // 2) | (a == nx // 2 - 1)
    return direct, fold & jnp.logical_not(near), fold & near


def sign_rows(count, chans):
    row = lax.broadcasted_iota(jnp.int32, (count, 1), 0)
    return jnp.where(row % chans < chans // 2, 1.0, -1.0)


def dot(left, right):
    return jnp.dot(left, right, preferred_element_type=f32)


def reversal(depth):
    row = lax.broadcasted_iota(jnp.int32, (depth, depth), 0)
    col = lax.broadcasted_iota(jnp.int32, (depth, depth), 1)
    return jnp.where(row + col == depth - 1, 1.0, 0.0).astype(bf16)


def shifted(rows):
    depth = rows.shape[1]
    lane = lax.broadcasted_iota(jnp.int32, rows.shape, 1)
    before = jnp.where(lane == 0, 0, pltpu.roll(rows, 1, 1)).astype(rows.dtype)
    after = jnp.where(lane == depth - 1, 0, pltpu.roll(rows, depth - 1, 1)).astype(rows.dtype)
    return jnp.concatenate([before, rows, after], axis=0)


def flat(block):
    return block.reshape(-1, block.shape[-1])


def weights_kernel(kernel, early, late, adjoint, blocks):
    chans = kernel.shape[3]
    wide = 2 * chans
    layers = early.shape[0] // (3 * wide)
    direct, fold_first, fold_second = place_flags()
    lane = lax.broadcasted_iota(jnp.int32, (wide, wide), 1)
    lane_sign = jnp.where(lane[:chans] % chans < chans // 2, 1.0, -1.0)
    signs = sign_rows(chans, chans) * lane_sign

    adjoint[...] = jnp.zeros(adjoint.shape, bf16)

    def tap(dx, dy, dz):
        return kernel[dx, dy, dz].astype(f32)

    for dx in range(3):
        for dy in range(3):
            for dz in range(3):
                turned = pltpu.roll(tap(2 - dx, 2 - dy, 2 - dz) * signs, chans, 1)
                block = jnp.concatenate([tap(dx, dy, dz), turned], axis=0)
                blocks[dx, dy, dz] = block
                other = pltpu.roll(tap(dx, dy, dz) * signs, chans, 1)
                column = jnp.concatenate([tap(2 - dx, 2 - dy, 2 - dz), other], axis=0)
                column = jnp.transpose(column)[:chans].astype(bf16)
                for x in range(layers):
                    rows = pl.ds((dy * layers + x) * chans, chans)
                    source = x + dx - 1
                    start = dz * layers * wide
                    if 0 <= source < layers:
                        adjoint[rows, start + source * wide : start + (source + 1) * wide] = column
                    else:
                        start += 3 * layers * wide
                        slot = jnp.where(direct, 0.0, 1.0) if source < 0 else jnp.where(direct, 1.0, 0.0)
                        adjoint[rows, start : start + wide] = (column * (1.0 - slot)).astype(bf16)
                        adjoint[rows, start + wide : start + 2 * wide] = (column * slot).astype(bf16)

    half = lane < chans

    def pair(left, right, left_kind, right_kind):
        left = jnp.where(left_kind, pltpu.roll(left, chans, 1), left)
        right = jnp.where(right_kind, right, pltpu.roll(right, chans, 1))
        return jnp.where(half, left, right).astype(bf16)

    none = jnp.zeros((wide, wide), f32)
    for dy in range(3):
        for x in range(layers):
            rows = pl.ds((dy * layers + x) * wide, wide)
            for dz in range(3):
                get = lambda dx: blocks[dx, dy, dz] if 0 <= dx < 3 else none
                start = dz * layers * chans
                for source in range(0, layers, 2):
                    ahead, next_ahead = get(source - x + 1), get(source + 1 - x + 1)
                    cols = slice(start + source * chans, start + (source + 2) * chans)
                    early[rows, cols] = pair(ahead, next_ahead, False, False)
                    late[rows, cols] = pair(ahead, next_ahead, True, True)
                start = 3 * layers * chans + dz * 2 * chans
                below, above = get(-x), get(layers - x + 1)
                first = jnp.where(direct, below, above)
                second = jnp.where(direct, above, below)
                cols = slice(start, start + 2 * chans)
                early[rows, cols] = pair(first, second, fold_first, fold_second)
                late[rows, cols] = pair(
                    first, second, jnp.logical_not(fold_first), jnp.logical_not(fold_second)
                )


def to_rows(natural, spread, x, rows):
    chans = natural.shape[0]
    whole = natural[:, x].astype(f32).reshape(chans * rows, natural.shape[3])
    for part in range(spread.shape[0]):
        spread[part] = whole[:, part * LANES : (part + 1) * LANES]


def row_from(spread, y, chans, rows):
    return jnp.concatenate(
        [spread[part, pl.ds(y, chans, stride=rows), :] for part in range(spread.shape[0])], axis=1
    )


def prepare_kernel(natural, given, image, spread):
    chans, layers, rows, depth = natural.shape
    flip = reversal(depth)
    signs = sign_rows(chans, chans)
    for x in range(layers):
        to_rows(natural, spread, x, rows)

        def body(y, carry):
            block = row_from(spread, y, chans, rows).astype(bf16)
            given[y, x] = block
            image[rows - 1 - y, layers - 1 - x] = (dot(block, flip) * signs).astype(bf16)
            return carry

        lax.fori_loop(0, rows, body, 0, unroll=4)


def emit_sides(read, rows, chans, layers, depth, signs, right, left):
    direct, fold_first, fold_second = place_flags()
    flip = reversal(depth)

    def write(target, upper, turned):
        @pl.when(turned)
        def _():
            def body(y, carry):
                block = jnp.where(upper, read(y, layers - 1), read(y, 0))
                block = (dot(block, flip) * signs).astype(bf16)
                if block.shape[0] != chans:
                    block = jnp.concatenate([block[chans:], block[:chans]], axis=0)
                target[rows - 1 - y] = block
                return carry

            lax.fori_loop(0, rows, body, 0, unroll=2)

        @pl.when(jnp.logical_not(turned))
        def _():
            def body(y, carry):
                target[y] = jnp.where(upper, read(y, layers - 1), read(y, 0))
                return carry

            lax.fori_loop(0, rows, body, 0, unroll=2)

    write(right, direct, fold_second)
    write(left, jnp.logical_not(direct), fold_first)


def sides_kernel(own, right, left):
    rows, layers, chans, depth = own.shape
    signs = sign_rows(chans, chans)
    emit_sides(lambda y, x: own[y, x], rows, chans, layers, depth, signs, right, left)


def accumulate(weights, own, first, second, total, fresh):
    rows = own.shape[0]
    outs = weights.shape[0] // 3

    def x3(y):
        return jnp.concatenate(
            [shifted(flat(own[y])), shifted(jnp.concatenate([first[y], second[y]], axis=0))], axis=0
        )

    def put(y, part, new):
        total[y] = part if new else total[y] + part

    part = dot(weights[:outs, :], x3(0))
    put(0, part, fresh)
    part = dot(weights[: 2 * outs, :], x3(1))
    put(1, part[:outs], fresh)
    put(0, part[outs:], False)

    def body(y, carry):
        part = dot(weights[...], x3(y))
        put(y, part[:outs], fresh)
        put(y - 1, part[outs : 2 * outs], False)
        put(y - 2, part[2 * outs :], False)
        return carry

    lax.fori_loop(2, rows - 2, body, 0, unroll=4)
    part = dot(weights[outs:, :], x3(rows - 2))
    put(rows - 3, part[:outs], False)
    put(rows - 4, part[outs:], False)
    part = dot(weights[2 * outs :, :], x3(rows - 1))
    put(rows - 3, part, False)


def early_kernel(weights, own, first, second, total):
    accumulate(weights, own, first, second, total, True)


def late_kernel(weights, own, first, second, partial, given, field, right, left, natural, total, spread):
    rows, layers, chans, depth = own.shape
    inner = rows - 2
    total[...] = partial[...]
    accumulate(weights, own, first, second, total, False)
    b, ny = lax.axis_index("ky"), lax.axis_size("ky")

    def body(y, carry):
        inside = ((y > 0) | (b > 0)) & ((y < inner - 1) | (b < ny - 1))
        both = jnp.concatenate([given[y + 1], own[y + 1]], axis=1)
        value = total[y].reshape(layers, 2 * chans, depth) - both.astype(f32)
        field[y] = jnp.where(inside, value, 0.0).astype(bf16)
        return carry

    lax.fori_loop(0, inner, body, 0, unroll=2)
    signs = sign_rows(2 * chans, chans)
    emit_sides(lambda y, x: field[y, x], inner, chans, layers, depth, signs, right, left)
    from_rows(lambda y, x: field[y + 1, x, :chans].astype(f32), natural, spread)


def from_rows(read, natural, spread):
    chans, layers, rows, _ = natural.shape
    for x in range(layers):

        def body(y, carry):
            row = read(y, x)
            for part in range(spread.shape[0]):
                spread[part, pl.ds(y, chans, stride=rows), :] = row[:, part * LANES : (part + 1) * LANES]
            return carry

        lax.fori_loop(0, rows, body, 0, unroll=4)
        for part in range(spread.shape[0]):
            natural[:, x, :, part * LANES : (part + 1) * LANES] = (
                spread[part].reshape(chans, rows, LANES).astype(bf16)
            )


def gradient_kernel(weights, field, first, second, given, mask, natural, total, spread):
    chans, _, _, _ = natural.shape
    accumulate(weights, field, first, second, total, True)

    def value(y, x):
        gradient = total[y, x * chans : (x + 1) * chans] - field[y + 1, x, :chans].astype(f32)
        keep = 1.0 - mask[pl.ds(y, 1)].astype(f32)
        return given[y + 2, x].astype(f32) - step_size * keep * gradient

    from_rows(value, natural, spread)


def call(kernel, shape, scratch, *args):
    return pl.pallas_call(
        kernel,
        out_shape=shape,
        scratch_shapes=scratch,
        compiler_params=pltpu.CompilerParams(vmem_limit_bytes=56 << 20),
    )(*args)


def like(*shape, dtype=bf16):
    return jax.ShapeDtypeStruct(shape, dtype)


def around_y(own):
    before, after = send(own[-2:], to_next), send(own[:2], to_previous)
    return jnp.concatenate([before, own, after], axis=0)


def around_x(own):
    rows, _, chans, depth = own.shape
    side = like(rows, chans, depth)
    right, left = call(sides_kernel, (side, side), [], own)
    return send(right, to_right), send(left, to_left)


def step(kspace, kernel, mask):
    chans, layers, rows, depth = kspace.shape
    wide = layers * 2 * chans
    block = like(rows, layers, chans, depth)
    spread = pltpu.VMEM((depth // LANES, chans * rows, LANES), f32)
    given, image = call(prepare_kernel, (block, block), [spread], kspace)
    virtual = send(image, to_mirror)

    square = like(3 * wide, 3 * (layers + 2) * chans)
    early, late, adjoint = call(
        weights_kernel,
        (square, square, like(3 * layers * chans, 3 * (layers + 2) * 2 * chans)),
        [pltpu.VMEM((3, 3, 3, 2 * chans, 2 * chans), f32)],
        kernel,
    )

    given = around_y(given)
    first, second = around_x(given)
    partial = call(
        early_kernel, like(rows + 2, wide, depth, dtype=f32), [], early, given, first, second
    )

    virtual = around_y(virtual)
    first, second = around_x(virtual)
    side = like(rows + 2, 2 * chans, depth)
    field, right, left, residual = call(
        late_kernel,
        (like(rows + 2, layers, 2 * chans, depth), side, side, like(chans, layers, rows, depth)),
        [pltpu.VMEM((rows + 2, wide, depth), f32), spread],
        late, virtual, first, second, partial, given,
    )
    first, second = send(right, to_right), send(left, to_left)
    updated = call(
        gradient_kernel,
        like(chans, layers, rows, depth),
        [pltpu.VMEM((rows, layers * chans, depth), f32), spread],
        adjoint, field, first, second, given, mask,
    )
    return updated, residual


def solution(mesh):
    spec = P(None, "kx", "ky", None)
    return jax.shard_map(
        step,
        mesh=mesh,
        in_specs=(spec, P(), P("ky", None)),
        out_specs=(spec, spec),
        check_vma=False,
    )
```

```python
import functools

import jax
import jax.numpy as jnp
from jax import lax
from jax.experimental import pallas as pl
from jax.experimental.pallas import tpu as pltpu
from jax.sharding import PartitionSpec as P


step_size = 0.5
LANES = 128
OUTER = 4
VMEM_LIMIT = 40 << 20
AXES = ("kx", "ky")
f32 = jnp.float32
bf16 = jnp.bfloat16


def on_line(a, b, nx, ny):
    inner = min(a, nx - 1 - a)
    return inner if b < ny // 2 else nx - 1 - inner


def line_device(a, b, nx, ny, place):
    near = b if b < ny // 2 else ny - 1 - b
    inner = min(place, nx - 1 - place)
    return (inner if a < nx // 2 else nx - 1 - inner), (near if place < nx // 2 else ny - 1 - near)


def to_mirror(a, b, nx, ny):
    return nx - 1 - a, ny - 1 - b


def to_right(a, b, nx, ny):
    place = on_line(a, b, nx, ny) + 1
    return line_device(a, b, nx, ny, place) if place < nx else None


def to_left(a, b, nx, ny):
    place = on_line(a, b, nx, ny) - 1
    return line_device(a, b, nx, ny, place) if place >= 0 else None


def to_next(a, b, nx, ny):
    return (a, b + 1) if b + 1 < ny else None


def to_previous(a, b, nx, ny):
    return (a, b - 1) if b > 0 else None


def send(value, move):
    nx, ny = lax.axis_size("kx"), lax.axis_size("ky")
    pairs = []
    for a in range(nx):
        for b in range(ny):
            target = move(a, b, nx, ny)
            if target is not None:
                pairs.append((a * ny + b, target[0] * ny + target[1]))
    return lax.ppermute(value, AXES, pairs)


def place_flags():
    a, b = lax.axis_index("kx"), lax.axis_index("ky")
    nx, ny = lax.axis_size("kx"), lax.axis_size("ky")
    near = b < ny // 2
    direct = near == (a < nx // 2)
    fold = (a == nx // 2) | (a == nx // 2 - 1)
    return direct, fold & jnp.logical_not(near), fold & near


def sign_rows(count, chans):
    row = lax.broadcasted_iota(jnp.int32, (count, 1), 0)
    return jnp.where(row % chans < chans // 2, 1.0, -1.0)


def dot(left, right):
    return jnp.dot(left, right, preferred_element_type=f32)


def reversal(depth):
    row = lax.broadcasted_iota(jnp.int32, (depth, depth), 0)
    col = lax.broadcasted_iota(jnp.int32, (depth, depth), 1)
    return jnp.where(row + col == depth - 1, 1.0, 0.0).astype(bf16)


def shifted(rows):
    depth = rows.shape[1]
    lane = lax.broadcasted_iota(jnp.int32, rows.shape, 1)
    before = jnp.where(lane == 0, 0, pltpu.roll(rows, 1, 1)).astype(rows.dtype)
    after = jnp.where(lane == depth - 1, 0, pltpu.roll(rows, depth - 1, 1)).astype(rows.dtype)
    return jnp.concatenate([before, rows, after], axis=0)


def flat(block):
    return block.reshape(-1, block.shape[-1])


def inside_y(y, count):
    b, ny = lax.axis_index("ky"), lax.axis_size("ky")
    return ((y > 0) | (b > 0)) & ((y < count - 1) | (b < ny - 1))


def weights_kernel(kernel, early, early_sides, late, late_sides, adjoint, outward, blocks, columns):
    chans = kernel.shape[3]
    wide = 2 * chans
    layers = early.shape[0] // (3 * wide)
    direct, fold_first, fold_second = place_flags()
    lane = lax.broadcasted_iota(jnp.int32, (wide, wide), 1)
    lane_sign = jnp.where(lane[:chans] % chans < chans // 2, 1.0, -1.0)
    signs = sign_rows(chans, chans) * lane_sign

    for dx in range(3):
        for dy in range(3):
            for dz in range(3):
                plain = kernel[dx, dy, dz].astype(f32)
                opposite = kernel[2 - dx, 2 - dy, 2 - dz].astype(f32)
                blocks[dx, dy, dz] = jnp.concatenate(
                    [plain, pltpu.roll(opposite * signs, chans, 1)], axis=0
                )
                column = jnp.concatenate([opposite, pltpu.roll(plain * signs, chans, 1)], axis=0)
                columns[dx, dy, dz] = jnp.transpose(column)[:chans]

    none = jnp.zeros((chans, wide), bf16)
    for dy in range(3):
        for x in range(layers):
            rows = pl.ds((dy * layers + x) * chans, chans)
            for dz in range(3):
                for source in range(layers):
                    dx = source - x + 1
                    start = (dz * layers + source) * wide
                    block = columns[dx, dy, dz].astype(bf16) if 0 <= dx < 3 else none
                    adjoint[rows, start : start + wide] = block
        for dz in range(3):
            rows, cols = pl.ds(dy * chans, chans), slice(dz * wide, (dz + 1) * wide)
            low, high = columns[0, dy, dz], columns[2, dy, dz]
            turn = lambda block: pltpu.roll(block, chans, 1) * lane_sign
            low_turned, high_turned = turn(columns[0, 2 - dy, 2 - dz]), turn(columns[2, 2 - dy, 2 - dz])
            right = jnp.where(direct, low, high)
            right = jnp.where(fold_second, jnp.where(direct, high_turned, low_turned), right)
            left = jnp.where(direct, high, low)
            left = jnp.where(fold_first, jnp.where(direct, low_turned, high_turned), left)
            outward[0, rows, cols] = right.astype(bf16)
            outward[1, rows, cols] = left.astype(bf16)

    half = lane < chans

    def pair(left, right, kind):
        left = jnp.where(kind, pltpu.roll(left, chans, 1), left)
        right = jnp.where(kind, right, pltpu.roll(right, chans, 1))
        return jnp.where(half, left, right).astype(bf16)

    empty = jnp.zeros((wide, wide), f32)
    for dy in range(3):
        for x in range(layers):
            rows = pl.ds((dy * layers + x) * wide, wide)
            for dz in range(3):
                get = lambda dx: blocks[dx, dy, dz] if 0 <= dx < 3 else empty
                start = dz * layers * chans
                for source in range(0, layers, 2):
                    ahead, behind = get(source - x + 1), get(source - x + 2)
                    cols = slice(start + source * chans, start + (source + 2) * chans)
                    early[rows, cols] = pair(ahead, behind, False)
                    late[rows, cols] = pair(ahead, behind, True)
        rows = pl.ds(dy * wide, wide)
        for slot, fold in ((0, fold_first), (1, fold_second)):
            lower = direct if slot == 0 else jnp.logical_not(direct)
            taps = [jnp.where(lower, blocks[0, dy, dz], blocks[2, dy, dz]) for dz in range(3)]
            for target, kind in ((early_sides, fold), (late_sides, jnp.logical_not(fold))):
                target[slot, rows, 0:wide] = pair(taps[0], taps[1], kind)
                target[slot, rows, wide : wide + chans] = pair(taps[2], taps[2], kind)[:, :chans]


def row_from(spread, y, chans, rows):
    return jnp.concatenate(
        [spread[part, pl.ds(y, chans, stride=rows), :] for part in range(spread.shape[0])], axis=1
    )


def prepare_kernel(natural, given, first_rows, last_rows, outer, inner, spread, turned):
    chans, layers, rows, depth = natural.shape
    flip = reversal(depth)
    signs = sign_rows(chans, chans)
    edge = outer.shape[0] // 2
    for x in range(layers):
        whole = natural[:, x].reshape(chans * rows, depth)
        mirrored = dot(whole, flip)
        whole = whole.astype(f32)
        for part in range(spread.shape[0]):
            spread[part] = whole[:, part * LANES : (part + 1) * LANES]
            turned[part] = mirrored[:, part * LANES : (part + 1) * LANES]
        for y in range(rows):
            block = row_from(spread, y, chans, rows).astype(bf16)
            given[y, x] = block
            if y < 2:
                first_rows[y, x] = block
            if y >= rows - 2:
                last_rows[y - rows + 2, x] = block
            target = rows - 1 - y
            block = (row_from(turned, y, chans, rows) * signs).astype(bf16)
            if target < edge:
                outer[target, layers - 1 - x] = block
            elif target < rows - edge:
                inner[target - edge, layers - 1 - x] = block
            else:
                outer[target - rows + 2 * edge, layers - 1 - x] = block


def emit_sides(read, rows, group, chans, depth, layers, signs, right, left):
    direct, fold_first, fold_second = place_flags()
    flip = reversal(depth)

    def write(target, upper, turned):
        def pick(y):
            return jnp.where(upper, read(y, layers - 1), read(y, 0))

        @pl.when(turned)
        def _():
            def body(j, carry):
                block = jnp.concatenate([pick(j * group + i).astype(bf16) for i in range(group)], axis=0)
                block = dot(block, flip)
                for i in range(group):
                    part = block[i * chans : (i + 1) * chans]
                    target[rows - 1 - j * group - i] = (part * signs).astype(bf16)
                return carry

            lax.fori_loop(0, rows // group, body, 0)

        @pl.when(jnp.logical_not(turned))
        def _():
            def body(y, carry):
                target[y] = pick(y).astype(bf16)
                return carry

            lax.fori_loop(0, rows, body, 0, unroll=2)

    write(right, direct, fold_second)
    write(left, jnp.logical_not(direct), fold_first)


def sides_kernel(layout, *refs):
    *segments, right, left, joined = refs
    rows, layers, chans, depth = joined.shape
    start = 0
    for index, offset, count in layout:
        joined[start : start + count] = segments[index][offset : offset + count]
        start += count
    signs = sign_rows(chans, chans)
    emit_sides(lambda y, x: joined[y, x], rows, 4, chans, depth, layers, signs, right, left)


def add_part(total, part, place, columns):
    outs = part.shape[0] // 3
    for third in range(3):
        target = place - third
        if isinstance(target, int) and not 0 <= target < total.shape[0]:
            continue
        total[target, columns] = total[target, columns] + part[third * outs : (third + 1) * outs]


def add_rows(weights, read, count, place, total, columns, static):
    def one(y, place):
        add_part(total, dot(weights[...], shifted(flat(read(y)))), place, columns)

    if static:
        for y in range(count):
            one(y, place + y)
    else:

        def body(y, carry):
            one(y, place + y)
            return carry

        lax.fori_loop(0, count, body, 0, unroll=4)


def side_columns(total, layers):
    direct, _, _ = place_flags()
    wide = total.shape[1] // layers
    upper = (layers - 1) * wide
    first = pl.multiple_of(jnp.where(direct, 0, upper), wide)
    second = pl.multiple_of(jnp.where(direct, upper, 0), wide)
    return pl.ds(first, wide), pl.ds(second, wide)


def add_own(weights, segments, total):
    for ref, count, offset, place, static in segments:
        add_rows(
            weights, lambda y, ref=ref, offset=offset: ref[y + offset], count, place, total,
            slice(None), static,
        )


def add_sides(weights, first, second, offset, count, place, total, columns, static):
    for slot, ref in ((0, first), (1, second)):
        add_rows(
            weights.at[slot], lambda y, ref=ref: ref[y + offset], count, place, total,
            columns[slot], static,
        )


def early_kernel(weights, top, own, bottom, total):
    rows = own.shape[0]
    total[...] = jnp.zeros(total.shape, f32)
    add_own(
        weights,
        ((top, 2, 0, 0, True), (own, rows, 0, 2, False), (bottom, 2, 0, rows + 2, True)),
        total,
    )


def middle_kernel(sides, first, second, partial, total):
    rows = total.shape[0] - 2
    layers = 3 * total.shape[1] // sides.shape[1]
    total[...] = partial[...]
    add_all_sides(sides, first, second, rows, total, side_columns(total, layers))


def add_all_sides(sides, first, second, rows, total, columns):
    for offset, count, static in ((0, 2, True), (2, rows, False), (rows + 2, 2, True)):
        add_sides(sides, first, second, offset, count, offset, total, columns, static)


def inner_kernel(weights, top, outer, inner, bottom, partial, total):
    rows = total.shape[0] - 2
    edge = outer.shape[0] // 2
    total[...] = partial[...]
    add_own(
        weights,
        (
            (top, 2, 0, 0, True),
            (outer, edge, 0, 2, True),
            (inner, rows - 2 * edge, 0, 2 + edge, False),
            (outer, edge, edge, rows + 2 - edge, True),
            (bottom, 2, 0, rows + 2, True),
        ),
        total,
    )


def residual_kernel(
    sides, outward, first, second, partial,
    top, given, bottom, virtual_top, virtual_outer, virtual_bottom, virtual_inner,
    field, right, left, total, reach,
):
    rows, layers, chans, depth = given.shape
    span = rows + 2
    edge = virtual_outer.shape[0] // 2
    total[...] = partial[...]
    columns = side_columns(total, layers)
    add_all_sides(sides, first, second, rows, total, columns)

    def finish(target, k, t):
        both = jnp.concatenate([k, t], axis=1).astype(f32)
        value = total[target].reshape(layers, 2 * chans, depth) - both
        field[target] = jnp.where(inside_y(target, span), value, 0.0).astype(bf16)

    def loop(count, first_target, k, t):
        def body(y, carry):
            finish(first_target + y, k(y), t(y))
            return carry

        lax.fori_loop(0, count, body, 0, unroll=2)

    finish(0, top[1], virtual_top[1])
    loop(edge, 1, lambda y: given[y], lambda y: virtual_outer[y])
    loop(rows - 2 * edge, 1 + edge, lambda y: given[y + edge], lambda y: virtual_inner[y])
    loop(edge, 1 + rows - edge, lambda y: given[y + rows - edge], lambda y: virtual_outer[y + edge])
    finish(span - 1, bottom[0], virtual_bottom[0])

    direct, _, _ = place_flags()
    reach[...] = jnp.zeros(reach.shape, f32)
    for slot, upper in ((0, direct), (1, jnp.logical_not(direct))):
        target, weights = reach.at[slot], outward.at[slot]

        def read(y, upper=upper):
            return jnp.where(upper, field[y, layers - 1], field[y, 0])

        add_rows(weights, read, 1, 0, target, slice(None), True)
        add_rows(weights, lambda y, read=read: read(y + 1), 1, 1, target, slice(None), True)
        add_rows(weights, lambda y, read=read: read(y + 2), rows - 2, 2, target, slice(None), False)
        add_rows(weights, lambda y, read=read: read(y + rows), 1, rows, target, slice(None), True)
        add_rows(weights, lambda y, read=read: read(y + rows + 1), 1, rows + 1, target, slice(None), True)
    ones = jnp.ones((chans, 1), f32)

    upper_reach = lambda y: jnp.where(direct, reach[0, y], reach[1, y])
    lower_reach = lambda y: jnp.where(direct, reach[1, y], reach[0, y])
    emit_sides(
        lambda y, x: upper_reach(y) if x == layers - 1 else lower_reach(y),
        rows, 4, chans, depth, layers, ones, right, left,
    )


def from_rows(read, natural, spread):
    chans, layers, rows, _ = natural.shape
    for x in range(layers):

        def body(y, carry):
            row = read(y, x)
            for part in range(spread.shape[0]):
                spread[part, pl.ds(y, chans, stride=rows), :] = row[:, part * LANES : (part + 1) * LANES]
            return carry

        lax.fori_loop(0, rows, body, 0, unroll=4)
        for part in range(spread.shape[0]):
            natural[:, x, :, part * LANES : (part + 1) * LANES] = (
                spread[part].reshape(chans, rows, LANES).astype(bf16)
            )


def own_gradient_kernel(weights, field, total, natural, spread):
    chans, _, rows, _ = natural.shape
    total[...] = jnp.zeros(total.shape, f32)
    add_own(
        weights,
        (
            (field, 1, 0, 0, True),
            (field, 1, 1, 1, True),
            (field, rows - 2, 2, 2, False),
            (field, 1, rows, rows, True),
            (field, 1, rows + 1, rows + 1, True),
        ),
        total,
    )
    from_rows(lambda y, x: field[y + 1, x, :chans].astype(f32), natural, spread)


def update_kernel(partial, first, second, field, given, mask, natural, spread):
    chans, layers, _, _ = natural.shape
    direct, _, _ = place_flags()

    def value(y, x):
        gradient = partial[y, x * chans : (x + 1) * chans] - field[y + 1, x, :chans].astype(f32)
        if x == 0:
            gradient += jnp.where(direct, first[y], second[y]).astype(f32)
        if x == layers - 1:
            gradient += jnp.where(direct, second[y], first[y]).astype(f32)
        keep = 1.0 - mask[pl.ds(y, 1)].astype(f32)
        return given[y, x].astype(f32) - step_size * keep * gradient

    from_rows(value, natural, spread)


def call(kernel, shape, scratch, *args):
    return pl.pallas_call(
        kernel,
        out_shape=shape,
        scratch_shapes=scratch,
        compiler_params=pltpu.CompilerParams(vmem_limit_bytes=VMEM_LIMIT),
    )(*args)


def like(*shape, dtype=bf16):
    return jax.ShapeDtypeStruct(shape, dtype)


def around_x(layout, *segments):
    rows = sum(count for _, _, count in layout)
    layers, chans, depth = segments[0].shape[1:]
    side = like(rows, chans, depth)
    joined = pltpu.VMEM((rows, layers, chans, depth), bf16)
    kernel = functools.partial(sides_kernel, layout)
    right, left = call(kernel, (side, side), [joined], *segments)
    return send(right, to_right), send(left, to_left)


def step(kspace, kernel, mask):
    chans, layers, rows, depth = kspace.shape
    wide = layers * 2 * chans
    edge = max(2, rows * OUTER // 32)
    block = lambda count: like(count, layers, chans, depth)
    spread = pltpu.VMEM((depth // LANES, chans * rows, LANES), f32)
    total = like(rows + 2, wide, depth, dtype=f32)

    given, head, tail, outer, inner = call(
        prepare_kernel,
        (block(rows), block(2), block(2), block(2 * edge), block(rows - 2 * edge)),
        [spread, spread],
        kspace,
    )
    top, bottom = send(tail, to_next), send(head, to_previous)
    outer = send(outer, to_mirror)
    inner = send(inner, to_mirror)
    layout = ((0, 0, 2), (1, 0, rows), (2, 0, 2))
    first, second = around_x(layout, top, given, bottom)

    early, early_sides, late, late_sides, adjoint, outward = call(
        weights_kernel,
        (
            like(3 * wide, 3 * layers * chans),
            like(2, 6 * chans, 3 * chans),
            like(3 * wide, 3 * layers * chans),
            like(2, 6 * chans, 3 * chans),
            like(3 * layers * chans, 3 * wide),
            like(2, 3 * chans, 6 * chans),
        ),
        [pltpu.VMEM((3, 3, 3, 2 * chans, 2 * chans), f32), pltpu.VMEM((3, 3, 3, chans, 2 * chans), f32)],
        kernel,
    )
    partial = call(early_kernel, total, [], early, top, given, bottom)

    virtual_top = send(outer[-2:], to_next)
    virtual_bottom = send(outer[:2], to_previous)
    partial = call(middle_kernel, total, [], early_sides, first, second, partial)

    layout = ((0, 0, 2), (1, 0, edge), (2, 0, rows - 2 * edge), (1, edge, edge), (3, 0, 2))
    first, second = around_x(layout, virtual_top, outer, inner, virtual_bottom)
    partial = call(
        inner_kernel, total, [], late, virtual_top, outer, inner, virtual_bottom, partial
    )
    side = like(rows, chans, depth)
    field, right, left = call(
        residual_kernel,
        (like(rows + 2, layers, 2 * chans, depth), side, side),
        [pltpu.VMEM(total.shape, f32), pltpu.VMEM((2, rows, chans, depth), f32)],
        late_sides, outward, first, second, partial,
        top, given, bottom, virtual_top, outer, virtual_bottom, inner,
    )
    first, second = send(right, to_right), send(left, to_left)
    natural = like(chans, layers, rows, depth)
    partial, residual = call(
        own_gradient_kernel,
        (like(rows, layers * chans, depth, dtype=f32), natural),
        [spread],
        adjoint, field,
    )
    updated = call(update_kernel, natural, [spread], partial, first, second, field, given, mask)
    return updated, residual


def solution(mesh):
    spec = P(None, "kx", "ky", None)
    return jax.shard_map(
        step,
        mesh=mesh,
        in_specs=(spec, P(), P("ky", None)),
        out_specs=(spec, spec),
        check_vma=False,
    )
```

```python
import functools

import jax
import jax.numpy as jnp
from jax import lax
from jax.experimental import pallas as pl
from jax.experimental.pallas import tpu as pltpu
from jax.sharding import PartitionSpec as P


step_size = 0.5
LANES = 128
OUTER = 4
MIDDLE = 6
VMEM_LIMIT = 40 << 20
AXES = ("kx", "ky")
f32 = jnp.float32
bf16 = jnp.bfloat16


def on_line(a, b, nx, ny):
    inner = min(a, nx - 1 - a)
    return inner if b < ny // 2 else nx - 1 - inner


def line_device(a, b, nx, ny, place):
    near = b if b < ny // 2 else ny - 1 - b
    inner = min(place, nx - 1 - place)
    return (inner if a < nx // 2 else nx - 1 - inner), (near if place < nx // 2 else ny - 1 - near)


def to_mirror(a, b, nx, ny):
    return nx - 1 - a, ny - 1 - b


def to_right(a, b, nx, ny):
    place = on_line(a, b, nx, ny) + 1
    return line_device(a, b, nx, ny, place) if place < nx else None


def to_left(a, b, nx, ny):
    place = on_line(a, b, nx, ny) - 1
    return line_device(a, b, nx, ny, place) if place >= 0 else None


def to_next(a, b, nx, ny):
    return (a, b + 1) if b + 1 < ny else None


def to_previous(a, b, nx, ny):
    return (a, b - 1) if b > 0 else None


def send(value, move):
    nx, ny = lax.axis_size("kx"), lax.axis_size("ky")
    pairs = []
    for a in range(nx):
        for b in range(ny):
            target = move(a, b, nx, ny)
            if target is not None:
                pairs.append((a * ny + b, target[0] * ny + target[1]))
    return lax.ppermute(value, AXES, pairs)


def place_flags():
    a, b = lax.axis_index("kx"), lax.axis_index("ky")
    nx, ny = lax.axis_size("kx"), lax.axis_size("ky")
    near = b < ny // 2
    direct = near == (a < nx // 2)
    fold = (a == nx // 2) | (a == nx // 2 - 1)
    return direct, fold & jnp.logical_not(near), fold & near


def sign_rows(count, chans):
    row = lax.broadcasted_iota(jnp.int32, (count, 1), 0)
    return jnp.where(row % chans < chans // 2, 1.0, -1.0)


def dot(left, right):
    return jnp.dot(left, right, preferred_element_type=f32)


def reversal(depth):
    row = lax.broadcasted_iota(jnp.int32, (depth, depth), 0)
    col = lax.broadcasted_iota(jnp.int32, (depth, depth), 1)
    return jnp.where(row + col == depth - 1, 1.0, 0.0).astype(bf16)


def shifted(rows):
    depth = rows.shape[1]
    lane = lax.broadcasted_iota(jnp.int32, rows.shape, 1)
    before = jnp.where(lane == 0, 0, pltpu.roll(rows, 1, 1)).astype(rows.dtype)
    after = jnp.where(lane == depth - 1, 0, pltpu.roll(rows, depth - 1, 1)).astype(rows.dtype)
    return jnp.concatenate([before, rows, after], axis=0)


def flat(block):
    return block.reshape(-1, block.shape[-1])


def inside_y(y, count):
    b, ny = lax.axis_index("ky"), lax.axis_size("ky")
    return ((y > 0) | (b > 0)) & ((y < count - 1) | (b < ny - 1))


def weights_kernel(kernel, early, early_sides, late, late_sides, adjoint, outward, blocks, columns):
    chans = kernel.shape[3]
    wide = 2 * chans
    layers = early.shape[0] // (3 * wide)
    direct, fold_first, fold_second = place_flags()
    lane = lax.broadcasted_iota(jnp.int32, (wide, wide), 1)
    lane_sign = jnp.where(lane[:chans] % chans < chans // 2, 1.0, -1.0)
    signs = sign_rows(chans, chans) * lane_sign

    for dx in range(3):
        for dy in range(3):
            for dz in range(3):
                plain = kernel[dx, dy, dz].astype(f32)
                opposite = kernel[2 - dx, 2 - dy, 2 - dz].astype(f32)
                blocks[dx, dy, dz] = jnp.concatenate(
                    [plain, pltpu.roll(opposite * signs, chans, 1)], axis=0
                )
                column = jnp.concatenate([opposite, pltpu.roll(plain * signs, chans, 1)], axis=0)
                columns[dx, dy, dz] = jnp.transpose(column)[:chans]

    none = jnp.zeros((chans, wide), bf16)
    for dy in range(3):
        for x in range(layers):
            rows = pl.ds((dy * layers + x) * chans, chans)
            for dz in range(3):
                for source in range(layers):
                    dx = source - x + 1
                    start = (dz * layers + source) * wide
                    block = columns[dx, dy, dz].astype(bf16) if 0 <= dx < 3 else none
                    adjoint[rows, start : start + wide] = block
        for dz in range(3):
            rows, cols = pl.ds(dy * chans, chans), slice(dz * wide, (dz + 1) * wide)
            low, high = columns[0, dy, dz], columns[2, dy, dz]
            turn = lambda block: pltpu.roll(block, chans, 1) * lane_sign
            low_turned, high_turned = turn(columns[0, 2 - dy, 2 - dz]), turn(columns[2, 2 - dy, 2 - dz])
            right = jnp.where(direct, low, high)
            right = jnp.where(fold_second, jnp.where(direct, high_turned, low_turned), right)
            left = jnp.where(direct, high, low)
            left = jnp.where(fold_first, jnp.where(direct, low_turned, high_turned), left)
            outward[0, rows, cols] = right.astype(bf16)
            outward[1, rows, cols] = left.astype(bf16)

    half = lane < chans

    def pair(left, right, kind):
        left = jnp.where(kind, pltpu.roll(left, chans, 1), left)
        right = jnp.where(kind, right, pltpu.roll(right, chans, 1))
        return jnp.where(half, left, right).astype(bf16)

    empty = jnp.zeros((wide, wide), f32)
    for dy in range(3):
        for x in range(layers):
            rows = pl.ds((dy * layers + x) * wide, wide)
            for dz in range(3):
                get = lambda dx: blocks[dx, dy, dz] if 0 <= dx < 3 else empty
                start = dz * layers * chans
                for source in range(0, layers, 2):
                    ahead, behind = get(source - x + 1), get(source - x + 2)
                    cols = slice(start + source * chans, start + (source + 2) * chans)
                    early[rows, cols] = pair(ahead, behind, False)
                    late[rows, cols] = pair(ahead, behind, True)
        rows = pl.ds(dy * wide, wide)
        for slot, fold in ((0, fold_first), (1, fold_second)):
            lower = direct if slot == 0 else jnp.logical_not(direct)
            taps = [jnp.where(lower, blocks[0, dy, dz], blocks[2, dy, dz]) for dz in range(3)]
            for target, kind in ((early_sides, fold), (late_sides, jnp.logical_not(fold))):
                target[slot, rows, 0:wide] = pair(taps[0], taps[1], kind)
                target[slot, rows, wide : wide + chans] = pair(taps[2], taps[2], kind)[:, :chans]


def row_from(spread, y, chans, rows):
    return jnp.concatenate(
        [spread[part, pl.ds(y, chans, stride=rows), :] for part in range(spread.shape[0])], axis=1
    )


def prepare_kernel(natural, given, first_rows, last_rows, outer, middle, inner, spread, turned):
    chans, layers, rows, depth = natural.shape
    flip = reversal(depth)
    signs = sign_rows(chans, chans)
    groups, start = [], 0
    for ref in (outer, middle):
        groups.append((ref, start, ref.shape[0] // 2))
        start += ref.shape[0] // 2
    for x in range(layers):
        whole = natural[:, x].reshape(chans * rows, depth)
        mirrored = dot(whole, flip)
        whole = whole.astype(f32)
        for part in range(spread.shape[0]):
            spread[part] = whole[:, part * LANES : (part + 1) * LANES]
            turned[part] = mirrored[:, part * LANES : (part + 1) * LANES]
        for y in range(rows):
            block = row_from(spread, y, chans, rows).astype(bf16)
            given[y, x] = block
            if y < 2:
                first_rows[y, x] = block
            if y >= rows - 2:
                last_rows[y - rows + 2, x] = block
            target = rows - 1 - y
            block = (row_from(turned, y, chans, rows) * signs).astype(bf16)
            for ref, start, half in groups:
                if start <= target < start + half:
                    ref[target - start, layers - 1 - x] = block
                if start <= rows - 1 - target < start + half:
                    ref[target - rows + start + 2 * half, layers - 1 - x] = block
            first_inner = (rows - inner.shape[0]) // 2
            if first_inner <= target < first_inner + inner.shape[0]:
                inner[target - first_inner, layers - 1 - x] = block


def emit_sides(read, rows, group, chans, depth, layers, signs, right, left):
    direct, fold_first, fold_second = place_flags()
    flip = reversal(depth)

    def write(target, upper, turned):
        def pick(y):
            return jnp.where(upper, read(y, layers - 1), read(y, 0))

        @pl.when(turned)
        def _():
            def body(j, carry):
                block = jnp.concatenate([pick(j * group + i).astype(bf16) for i in range(group)], axis=0)
                block = dot(block, flip)
                for i in range(group):
                    part = block[i * chans : (i + 1) * chans]
                    target[rows - 1 - j * group - i] = (part * signs).astype(bf16)
                return carry

            lax.fori_loop(0, rows // group, body, 0)

        @pl.when(jnp.logical_not(turned))
        def _():
            def body(y, carry):
                target[y] = pick(y).astype(bf16)
                return carry

            lax.fori_loop(0, rows, body, 0, unroll=2)

    write(right, direct, fold_second)
    write(left, jnp.logical_not(direct), fold_first)


def sides_kernel(layout, *refs):
    *segments, right, left, joined = refs
    rows, layers, chans, depth = joined.shape
    start = 0
    for index, offset, count in layout:
        joined[start : start + count] = segments[index][offset : offset + count]
        start += count
    signs = sign_rows(chans, chans)
    emit_sides(lambda y, x: joined[y, x], rows, 2, chans, depth, layers, signs, right, left)


def add_part(total, part, place, columns):
    outs = part.shape[0] // 3
    for third in range(3):
        target = place - third
        if isinstance(target, int) and not 0 <= target < total.shape[0]:
            continue
        total[target, columns] = total[target, columns] + part[third * outs : (third + 1) * outs]


def add_rows(weights, read, count, place, total, columns, static):
    def one(y, place):
        add_part(total, dot(weights[...], shifted(flat(read(y)))), place, columns)

    if static:
        for y in range(count):
            one(y, place + y)
    else:

        def body(y, carry):
            one(y, place + y)
            return carry

        lax.fori_loop(0, count, body, 0, unroll=4)


def side_columns(total, layers):
    direct, _, _ = place_flags()
    wide = total.shape[1] // layers
    upper = (layers - 1) * wide
    first = pl.multiple_of(jnp.where(direct, 0, upper), wide)
    second = pl.multiple_of(jnp.where(direct, upper, 0), wide)
    return pl.ds(first, wide), pl.ds(second, wide)


def add_own(weights, segments, total):
    for ref, count, offset, place, static in segments:
        add_rows(
            weights, lambda y, ref=ref, offset=offset: ref[y + offset], count, place, total,
            slice(None), static,
        )


def add_sides(weights, first, second, offset, count, place, total, columns, static):
    for slot, ref in ((0, first), (1, second)):
        add_rows(
            weights.at[slot], lambda y, ref=ref: ref[y + offset], count, place, total,
            columns[slot], static,
        )


def early_kernel(weights, own, total):
    total[...] = jnp.zeros(total.shape, f32)
    add_own(weights, ((own, own.shape[0], 0, 2, False),), total)


def given_kernel(sides, first, second, partial, total):
    rows = total.shape[0] - 2
    layers = 3 * total.shape[1] // sides.shape[1]
    total[...] = partial[...]
    add_sides(sides, first, second, 0, rows, 2, total, side_columns(total, layers), False)


def outer_kernel(early, late, top, bottom, outer, middle, partial, total):
    rows = total.shape[0] - 2
    edge, half = outer.shape[0] // 2, middle.shape[0] // 2
    total[...] = partial[...]
    add_own(early, ((top, 2, 0, 0, True), (bottom, 2, 0, rows + 2, True)), total)
    add_own(
        late,
        (
            (outer, edge, 0, 2, True),
            (middle, half, 0, 2 + edge, True),
            (middle, half, half, rows + 2 - edge - half, True),
            (outer, edge, edge, rows + 2 - edge, True),
        ),
        total,
    )


def middle_kernel(early_sides, late_sides, first, second, partial, total):
    rows = total.shape[0] - 2
    half = (first.shape[0] - 4) // 2
    columns = side_columns(total, 3 * total.shape[1] // early_sides.shape[1])
    total[...] = partial[...]
    for offset, place in ((0, 0), (2 + 2 * half, rows + 2)):
        add_sides(early_sides, first, second, offset, 2, place, total, columns, True)
    for offset, place in ((2, 2), (2 + half, rows + 2 - half)):
        add_sides(late_sides, first, second, offset, half, place, total, columns, True)


def inner_kernel(weights, top, inner, bottom, partial, total):
    rows = total.shape[0] - 2
    count = inner.shape[0]
    total[...] = partial[...]
    add_own(
        weights,
        (
            (top, 2, 0, 0, True),
            (inner, count, 0, 2 + (rows - count) // 2, True),
            (bottom, 2, 0, rows + 2, True),
        ),
        total,
    )


def residual_kernel(
    sides, outward, first, second, partial,
    top, given, bottom, virtual_top, virtual_outer, virtual_middle, virtual_bottom, virtual_inner,
    field, right, left, total, reach,
):
    rows, layers, chans, depth = given.shape
    span = rows + 2
    edge, half = virtual_outer.shape[0] // 2, virtual_middle.shape[0] // 2
    inner = rows - 2 * edge - 2 * half
    total[...] = partial[...]
    columns = side_columns(total, layers)
    for offset, count, place in ((0, 2, 0), (2, inner, 2 + edge + half), (2 + inner, 2, rows + 2)):
        add_sides(sides, first, second, offset, count, place, total, columns, True)

    def finish(target, k, t):
        both = jnp.concatenate([k, t], axis=1).astype(f32)
        value = total[target].reshape(layers, 2 * chans, depth) - both
        field[target] = jnp.where(inside_y(target, span), value, 0.0).astype(bf16)

    def loop(count, first_target, k, t):
        def body(y, carry):
            finish(first_target + y, k(y), t(y))
            return carry

        lax.fori_loop(0, count, body, 0, unroll=2)

    finish(0, top[1], virtual_top[1])
    y = 0
    for ref, offset, count in (
        (virtual_outer, 0, edge), (virtual_middle, 0, half), (virtual_inner, 0, inner),
        (virtual_middle, half, half), (virtual_outer, edge, edge),
    ):
        loop(
            count, 1 + y, lambda j, y=y: given[j + y],
            lambda j, ref=ref, offset=offset: ref[j + offset],
        )
        y += count
    finish(span - 1, bottom[0], virtual_bottom[0])

    direct, _, _ = place_flags()
    reach[...] = jnp.zeros(reach.shape, f32)
    for slot, upper in ((0, direct), (1, jnp.logical_not(direct))):
        target, weights = reach.at[slot], outward.at[slot]

        def read(y, upper=upper):
            return jnp.where(upper, field[y, layers - 1], field[y, 0])

        add_rows(weights, read, 1, 0, target, slice(None), True)
        add_rows(weights, lambda y, read=read: read(y + 1), 1, 1, target, slice(None), True)
        add_rows(weights, lambda y, read=read: read(y + 2), rows - 2, 2, target, slice(None), False)
        add_rows(weights, lambda y, read=read: read(y + rows), 1, rows, target, slice(None), True)
        add_rows(weights, lambda y, read=read: read(y + rows + 1), 1, rows + 1, target, slice(None), True)
    ones = jnp.ones((chans, 1), f32)

    upper_reach = lambda y: jnp.where(direct, reach[0, y], reach[1, y])
    lower_reach = lambda y: jnp.where(direct, reach[1, y], reach[0, y])
    emit_sides(
        lambda y, x: upper_reach(y) if x == layers - 1 else lower_reach(y),
        rows, 4, chans, depth, layers, ones, right, left,
    )


def from_rows(read, natural, spread):
    chans, layers, rows, _ = natural.shape
    for x in range(layers):

        def body(y, carry):
            row = read(y, x)
            for part in range(spread.shape[0]):
                spread[part, pl.ds(y, chans, stride=rows), :] = row[:, part * LANES : (part + 1) * LANES]
            return carry

        lax.fori_loop(0, rows, body, 0, unroll=4)
        for part in range(spread.shape[0]):
            natural[:, x, :, part * LANES : (part + 1) * LANES] = (
                spread[part].reshape(chans, rows, LANES).astype(bf16)
            )


def own_gradient_kernel(weights, field, total, natural, spread):
    chans, _, rows, _ = natural.shape
    total[...] = jnp.zeros(total.shape, f32)
    add_own(
        weights,
        (
            (field, 1, 0, 0, True),
            (field, 1, 1, 1, True),
            (field, rows - 2, 2, 2, False),
            (field, 1, rows, rows, True),
            (field, 1, rows + 1, rows + 1, True),
        ),
        total,
    )
    from_rows(lambda y, x: field[y + 1, x, :chans].astype(f32), natural, spread)


def update_kernel(partial, first, second, field, given, mask, natural, spread):
    chans, layers, _, _ = natural.shape
    direct, _, _ = place_flags()

    def value(y, x):
        gradient = partial[y, x * chans : (x + 1) * chans] - field[y + 1, x, :chans].astype(f32)
        if x == 0:
            gradient += jnp.where(direct, first[y], second[y]).astype(f32)
        if x == layers - 1:
            gradient += jnp.where(direct, second[y], first[y]).astype(f32)
        keep = 1.0 - mask[pl.ds(y, 1)].astype(f32)
        return given[y, x].astype(f32) - step_size * keep * gradient

    from_rows(value, natural, spread)


def call(kernel, shape, scratch, *args):
    return pl.pallas_call(
        kernel,
        out_shape=shape,
        scratch_shapes=scratch,
        compiler_params=pltpu.CompilerParams(vmem_limit_bytes=VMEM_LIMIT),
    )(*args)


def like(*shape, dtype=bf16):
    return jax.ShapeDtypeStruct(shape, dtype)


def around_x(layout, *segments):
    rows = sum(count for _, _, count in layout)
    layers, chans, depth = segments[0].shape[1:]
    side = like(rows, chans, depth)
    joined = pltpu.VMEM((rows, layers, chans, depth), bf16)
    kernel = functools.partial(sides_kernel, layout)
    right, left = call(kernel, (side, side), [joined], *segments)
    return send(right, to_right), send(left, to_left)


def step(kspace, kernel, mask):
    chans, layers, rows, depth = kspace.shape
    wide = layers * 2 * chans
    edge = max(2, rows * OUTER // 32)
    half = max(1, rows * MIDDLE // 32)
    count = rows - 2 * edge - 2 * half
    block = lambda size: like(size, layers, chans, depth)
    spread = pltpu.VMEM((depth // LANES, chans * rows, LANES), f32)
    total = like(rows + 2, wide, depth, dtype=f32)

    given, head, tail, outer, middle, inner = call(
        prepare_kernel,
        (block(rows), block(2), block(2), block(2 * edge), block(2 * half), block(count)),
        [spread, spread],
        kspace,
    )
    outer = send(outer, to_mirror)
    given_sides = around_x(((0, 0, rows),), given)
    middle = send(middle, to_mirror)
    top, bottom = send(tail, to_next), send(head, to_previous)
    inner = send(inner, to_mirror)

    early, early_sides, late, late_sides, adjoint, outward = call(
        weights_kernel,
        (
            like(3 * wide, 3 * layers * chans),
            like(2, 6 * chans, 3 * chans),
            like(3 * wide, 3 * layers * chans),
            like(2, 6 * chans, 3 * chans),
            like(3 * layers * chans, 3 * wide),
            like(2, 3 * chans, 6 * chans),
        ),
        [pltpu.VMEM((3, 3, 3, 2 * chans, 2 * chans), f32), pltpu.VMEM((3, 3, 3, chans, 2 * chans), f32)],
        kernel,
    )
    partial = call(early_kernel, total, [], early, given)
    partial = call(given_kernel, total, [], early_sides, *given_sides, partial)

    virtual_top = send(outer[-2:], to_next)
    virtual_bottom = send(outer[:2], to_previous)
    layout = (
        (0, 0, 2), (1, 0, edge), (2, 0, half), (2, half, half), (1, edge, edge), (3, 0, 2)
    )
    first, second = around_x(layout, top, outer, middle, bottom)
    partial = call(outer_kernel, total, [], early, late, top, bottom, outer, middle, partial)
    middle_sides = first, second

    layout = ((0, 0, 2), (1, 0, count), (2, 0, 2))
    first, second = around_x(layout, virtual_top, inner, virtual_bottom)
    partial = call(inner_kernel, total, [], late, virtual_top, inner, virtual_bottom, partial)
    partial = call(middle_kernel, total, [], early_sides, late_sides, *middle_sides, partial)
    side = like(rows, chans, depth)
    field, right, left = call(
        residual_kernel,
        (like(rows + 2, layers, 2 * chans, depth), side, side),
        [pltpu.VMEM(total.shape, f32), pltpu.VMEM((2, rows, chans, depth), f32)],
        late_sides, outward, first, second, partial,
        top, given, bottom, virtual_top, outer, middle, virtual_bottom, inner,
    )
    first, second = send(right, to_right), send(left, to_left)
    natural = like(chans, layers, rows, depth)
    partial, residual = call(
        own_gradient_kernel,
        (like(rows, layers * chans, depth, dtype=f32), natural),
        [spread],
        adjoint, field,
    )
    updated = call(update_kernel, natural, [spread], partial, first, second, field, given, mask)
    return updated, residual


def solution(mesh):
    spec = P(None, "kx", "ky", None)
    return jax.shard_map(
        step,
        mesh=mesh,
        in_specs=(spec, P(), P("ky", None)),
        out_specs=(spec, spec),
        check_vma=False,
    )
```

```python
import functools

import jax
import jax.numpy as jnp
from jax import lax
from jax.experimental import pallas as pl
from jax.experimental.pallas import tpu as pltpu
from jax.sharding import PartitionSpec as P


step_size = 0.5
LANES = 128
IN_VMEM = pl.BlockSpec(memory_space=pltpu.VMEM)
OUTER = 4
MIDDLE = 8
VMEM_LIMIT = 40 << 20
AXES = ("kx", "ky")
f32 = jnp.float32
bf16 = jnp.bfloat16


def on_line(a, b, nx, ny):
    inner = min(a, nx - 1 - a)
    return inner if b < ny // 2 else nx - 1 - inner


def line_device(a, b, nx, ny, place):
    near = b if b < ny // 2 else ny - 1 - b
    inner = min(place, nx - 1 - place)
    return (inner if a < nx // 2 else nx - 1 - inner), (near if place < nx // 2 else ny - 1 - near)


def to_mirror(a, b, nx, ny):
    return nx - 1 - a, ny - 1 - b


def to_right(a, b, nx, ny):
    place = on_line(a, b, nx, ny) + 1
    return line_device(a, b, nx, ny, place) if place < nx else None


def to_left(a, b, nx, ny):
    place = on_line(a, b, nx, ny) - 1
    return line_device(a, b, nx, ny, place) if place >= 0 else None


def to_next(a, b, nx, ny):
    return (a, b + 1) if b + 1 < ny else None


def to_previous(a, b, nx, ny):
    return (a, b - 1) if b > 0 else None


def send(value, move):
    nx, ny = lax.axis_size("kx"), lax.axis_size("ky")
    pairs = []
    for a in range(nx):
        for b in range(ny):
            target = move(a, b, nx, ny)
            if target is not None:
                pairs.append((a * ny + b, target[0] * ny + target[1]))
    return lax.ppermute(value, AXES, pairs)


def place_flags():
    a, b = lax.axis_index("kx"), lax.axis_index("ky")
    nx, ny = lax.axis_size("kx"), lax.axis_size("ky")
    near = b < ny // 2
    direct = near == (a < nx // 2)
    fold = (a == nx // 2) | (a == nx // 2 - 1)
    return direct, fold & jnp.logical_not(near), fold & near


def sign_rows(count, chans):
    row = lax.broadcasted_iota(jnp.int32, (count, 1), 0)
    return jnp.where(row % chans < chans // 2, 1.0, -1.0)


def dot(left, right):
    return jnp.dot(left, right, preferred_element_type=f32)


def reversal(depth):
    row = lax.broadcasted_iota(jnp.int32, (depth, depth), 0)
    col = lax.broadcasted_iota(jnp.int32, (depth, depth), 1)
    return jnp.where(row + col == depth - 1, 1.0, 0.0).astype(bf16)


def shifted(rows):
    depth = rows.shape[1]
    lane = lax.broadcasted_iota(jnp.int32, rows.shape, 1)
    before = jnp.where(lane == 0, 0, pltpu.roll(rows, 1, 1)).astype(rows.dtype)
    after = jnp.where(lane == depth - 1, 0, pltpu.roll(rows, depth - 1, 1)).astype(rows.dtype)
    return jnp.concatenate([before, rows, after], axis=0)


def flat(block):
    return block.reshape(-1, block.shape[-1])


def inside_y(y, count):
    b, ny = lax.axis_index("ky"), lax.axis_size("ky")
    return ((y > 0) | (b > 0)) & ((y < count - 1) | (b < ny - 1))


def weights_kernel(kernel, early, early_sides, late, late_sides, adjoint, outward, blocks, columns):
    chans = kernel.shape[3]
    wide = 2 * chans
    layers = early.shape[0] // (3 * wide)
    direct, fold_first, fold_second = place_flags()
    lane = lax.broadcasted_iota(jnp.int32, (wide, wide), 1)
    lane_sign = jnp.where(lane[:chans] % chans < chans // 2, 1.0, -1.0)
    signs = sign_rows(chans, chans) * lane_sign

    for dx in range(3):
        for dy in range(3):
            for dz in range(3):
                plain = kernel[dx, dy, dz].astype(f32)
                opposite = kernel[2 - dx, 2 - dy, 2 - dz].astype(f32)
                blocks[dx, dy, dz] = jnp.concatenate(
                    [plain, pltpu.roll(opposite * signs, chans, 1)], axis=0
                )
                column = jnp.concatenate([opposite, pltpu.roll(plain * signs, chans, 1)], axis=0)
                columns[dx, dy, dz] = jnp.transpose(column)[:chans]

    none = jnp.zeros((chans, wide), bf16)
    for dy in range(3):
        for x in range(layers):
            rows = pl.ds((dy * layers + x) * chans, chans)
            for dz in range(3):
                for source in range(layers):
                    dx = source - x + 1
                    start = (dz * layers + source) * wide
                    block = columns[dx, dy, dz].astype(bf16) if 0 <= dx < 3 else none
                    adjoint[rows, start : start + wide] = block
        for dz in range(3):
            rows, cols = pl.ds(dy * chans, chans), slice(dz * wide, (dz + 1) * wide)
            low, high = columns[0, dy, dz], columns[2, dy, dz]
            turn = lambda block: pltpu.roll(block, chans, 1) * lane_sign
            low_turned, high_turned = turn(columns[0, 2 - dy, 2 - dz]), turn(columns[2, 2 - dy, 2 - dz])
            right = jnp.where(direct, low, high)
            right = jnp.where(fold_second, jnp.where(direct, high_turned, low_turned), right)
            left = jnp.where(direct, high, low)
            left = jnp.where(fold_first, jnp.where(direct, low_turned, high_turned), left)
            outward[0, rows, cols] = right.astype(bf16)
            outward[1, rows, cols] = left.astype(bf16)

    half = lane < chans

    def pair(left, right, kind):
        left = jnp.where(kind, pltpu.roll(left, chans, 1), left)
        right = jnp.where(kind, right, pltpu.roll(right, chans, 1))
        return jnp.where(half, left, right).astype(bf16)

    empty = jnp.zeros((wide, wide), f32)
    for dy in range(3):
        for x in range(layers):
            rows = pl.ds((dy * layers + x) * wide, wide)
            for dz in range(3):
                get = lambda dx: blocks[dx, dy, dz] if 0 <= dx < 3 else empty
                start = dz * layers * chans
                for source in range(0, layers, 2):
                    ahead, behind = get(source - x + 1), get(source - x + 2)
                    cols = slice(start + source * chans, start + (source + 2) * chans)
                    early[rows, cols] = pair(ahead, behind, False)
                    late[rows, cols] = pair(ahead, behind, True)
        rows = pl.ds(dy * wide, wide)
        for slot, fold in ((0, fold_first), (1, fold_second)):
            lower = direct if slot == 0 else jnp.logical_not(direct)
            taps = [jnp.where(lower, blocks[0, dy, dz], blocks[2, dy, dz]) for dz in range(3)]
            for target, kind in ((early_sides, fold), (late_sides, jnp.logical_not(fold))):
                target[slot, rows, 0:wide] = pair(taps[0], taps[1], kind)
                target[slot, rows, wide : wide + chans] = pair(taps[2], taps[2], kind)[:, :chans]


def row_from(spread, y, chans, rows):
    return jnp.concatenate(
        [spread[part, pl.ds(y, chans, stride=rows), :] for part in range(spread.shape[0])], axis=1
    )


def prepare_kernel(natural, given, first_rows, last_rows, outer, middle, inner, spread, turned):
    chans, layers, rows, depth = natural.shape
    flip = reversal(depth)
    signs = sign_rows(chans, chans)
    groups, start = [], 0
    for ref in (outer, middle):
        groups.append((ref, start, ref.shape[0] // 2))
        start += ref.shape[0] // 2
    for x in range(layers):
        whole = natural[:, x].reshape(chans * rows, depth)
        mirrored = dot(whole, flip)
        whole = whole.astype(f32)
        for part in range(spread.shape[0]):
            spread[part] = whole[:, part * LANES : (part + 1) * LANES]
            turned[part] = mirrored[:, part * LANES : (part + 1) * LANES]
        for y in range(rows):
            block = row_from(spread, y, chans, rows).astype(bf16)
            given[y, x] = block
            if y < 2:
                first_rows[y, x] = block
            if y >= rows - 2:
                last_rows[y - rows + 2, x] = block
            target = rows - 1 - y
            block = (row_from(turned, y, chans, rows) * signs).astype(bf16)
            for ref, start, half in groups:
                if start <= target < start + half:
                    ref[target - start, layers - 1 - x] = block
                if start <= rows - 1 - target < start + half:
                    ref[target - rows + start + 2 * half, layers - 1 - x] = block
            first_inner = (rows - inner.shape[0]) // 2
            if first_inner <= target < first_inner + inner.shape[0]:
                inner[target - first_inner, layers - 1 - x] = block


def emit_sides(read, rows, group, chans, depth, layers, signs, right, left):
    direct, fold_first, fold_second = place_flags()
    flip = reversal(depth)

    def write(target, upper, turned):
        def pick(y):
            return jnp.where(upper, read(y, layers - 1), read(y, 0))

        @pl.when(turned)
        def _():
            def body(j, carry):
                block = jnp.concatenate([pick(j * group + i).astype(bf16) for i in range(group)], axis=0)
                block = dot(block, flip)
                for i in range(group):
                    part = block[i * chans : (i + 1) * chans]
                    target[rows - 1 - j * group - i] = (part * signs).astype(bf16)
                return carry

            lax.fori_loop(0, rows // group, body, 0)

        @pl.when(jnp.logical_not(turned))
        def _():
            def body(y, carry):
                target[y] = pick(y).astype(bf16)
                return carry

            lax.fori_loop(0, rows, body, 0, unroll=2)

    write(right, direct, fold_second)
    write(left, jnp.logical_not(direct), fold_first)


def sides_kernel(layout, *refs):
    *segments, right, left, joined = refs
    rows, layers, chans, depth = joined.shape
    start = 0
    for index, offset, count in layout:
        joined[start : start + count] = segments[index][offset : offset + count]
        start += count
    signs = sign_rows(chans, chans)
    emit_sides(lambda y, x: joined[y, x], rows, 2 if rows % 4 else 4, chans, depth, layers, signs, right, left)


def add_part(total, part, place, columns):
    outs = part.shape[0] // 3
    for third in range(3):
        target = place - third
        if isinstance(target, int) and not 0 <= target < total.shape[0]:
            continue
        total[target, columns] = total[target, columns] + part[third * outs : (third + 1) * outs]


def add_rows(weights, read, count, place, total, columns, static):
    def one(y, place):
        add_part(total, dot(weights[...], shifted(flat(read(y)))), place, columns)

    if static:
        for y in range(count):
            one(y, place + y)
    else:

        def body(y, carry):
            one(y, place + y)
            return carry

        lax.fori_loop(0, count, body, 0, unroll=4)


def side_columns(total, layers):
    direct, _, _ = place_flags()
    wide = total.shape[1] // layers
    upper = (layers - 1) * wide
    first = pl.multiple_of(jnp.where(direct, 0, upper), wide)
    second = pl.multiple_of(jnp.where(direct, upper, 0), wide)
    return pl.ds(first, wide), pl.ds(second, wide)


def add_own(weights, segments, total):
    for ref, count, offset, place, static in segments:
        add_rows(
            weights, lambda y, ref=ref, offset=offset: ref[y + offset], count, place, total,
            slice(None), static,
        )


def add_sides(weights, first, second, offset, count, place, total, columns, static):
    def one(y, place):
        for slot, ref in ((0, first), (1, second)):
            part = dot(weights[slot], shifted(flat(ref[y + offset])))
            add_part(total, part, place, columns[slot])

    if static:
        for y in range(count):
            one(y, place + y)
    else:

        def body(y, carry):
            one(y, place + y)
            return carry

        lax.fori_loop(0, count, body, 0, unroll=4)


def early_kernel(weights, own, total):
    total[...] = jnp.zeros(total.shape, f32)
    add_own(weights, ((own, own.shape[0], 0, 2, False),), total)


def given_kernel(sides, first, second, partial, total):
    rows = total.shape[0] - 2
    layers = 3 * total.shape[1] // sides.shape[1]
    add_sides(sides, first, second, 0, rows, 2, total, side_columns(total, layers), False)


def outer_kernel(early, late, top, bottom, outer, partial, total):
    end, edge = total.shape[0], outer.shape[0] // 2
    add_own(early, ((top, 2, 0, 0, True), (bottom, 2, 0, end, True)), total)
    add_own(
        late,
        (
            (outer, edge, 0, 2, True),
            (outer, edge, edge, end - edge, True),
        ),
        total,
    )


def outer_rows(rows):
    return max(2, rows * OUTER // 32)


def own_kernel(late, virtual_top, middle, virtual_bottom, partial, total):
    end, half = total.shape[0], middle.shape[0] // 2
    edge = outer_rows(end - 2)
    add_own(
        late,
        (
            (virtual_top, 2, 0, 0, True),
            (middle, half, 0, 2 + edge, True),
            (middle, half, half, end - edge - half, True),
            (virtual_bottom, 2, 0, end, True),
        ),
        total,
    )


def inner_kernel(
    late, early_sides, late_sides, inner,
    first_outer, second_outer, first_middle, second_middle, partial, total,
):
    end, edge, half = total.shape[0], first_outer.shape[0] // 2 - 2, first_middle.shape[0] // 2
    add_own(late, ((inner, inner.shape[0], 0, 2 + edge + half, True),), total)
    columns = side_columns(total, 3 * total.shape[1] // early_sides.shape[1])
    for weights, first, second, offset, size, place in (
        (early_sides, first_outer, second_outer, 0, 2, 0),
        (late_sides, first_outer, second_outer, 2, edge, 2),
        (late_sides, first_outer, second_outer, 2 + edge, edge, end - edge),
        (early_sides, first_outer, second_outer, 2 + 2 * edge, 2, end),
        (late_sides, first_middle, second_middle, 0, half, 2 + edge),
        (late_sides, first_middle, second_middle, half, half, end - edge - half),
    ):
        add_sides(weights, first, second, offset, size, place, total, columns, True)


def residual_kernel(
    sides, outward, first, second, partial,
    top, given, bottom, virtual_top, virtual_outer, virtual_middle, virtual_bottom, virtual_inner,
    total, field, right, left, reach,
):
    rows, layers, chans, depth = given.shape
    span = rows + 2
    edge, half = virtual_outer.shape[0] // 2, virtual_middle.shape[0] // 2
    inner = rows - 2 * edge - 2 * half
    columns = side_columns(total, layers)
    for offset, count, place in ((0, 2, 0), (2, inner, 2 + edge + half), (2 + inner, 2, rows + 2)):
        add_sides(sides, first, second, offset, count, place, total, columns, True)

    def finish(target, k, t):
        both = jnp.concatenate([k, t], axis=1).astype(f32)
        value = total[target].reshape(layers, 2 * chans, depth) - both
        field[target] = jnp.where(inside_y(target, span), value, 0.0).astype(bf16)

    def loop(count, first_target, k, t):
        def body(y, carry):
            finish(first_target + y, k(y), t(y))
            return carry

        lax.fori_loop(0, count, body, 0, unroll=2)

    finish(0, top[1], virtual_top[1])
    y = 0
    for ref, offset, count in (
        (virtual_outer, 0, edge), (virtual_middle, 0, half), (virtual_inner, 0, inner),
        (virtual_middle, half, half), (virtual_outer, edge, edge),
    ):
        loop(
            count, 1 + y, lambda j, y=y: given[j + y],
            lambda j, ref=ref, offset=offset: ref[j + offset],
        )
        y += count
    finish(span - 1, bottom[0], virtual_bottom[0])

    direct, _, _ = place_flags()
    reach[...] = jnp.zeros(reach.shape, f32)

    def add_reach(y, place):
        upper, lower = field[y, layers - 1], field[y, 0]
        for slot, row in (
            (0, jnp.where(direct, upper, lower)), (1, jnp.where(direct, lower, upper))
        ):
            add_part(reach.at[slot], dot(outward[slot], shifted(row)), place, slice(None))

    def body(y, carry):
        add_reach(y, y)
        return carry

    for y in (0, 1):
        add_reach(y, y)
    lax.fori_loop(2, rows, body, 0, unroll=7 if (rows - 2) % 7 == 0 else 2)
    for y in (rows, rows + 1):
        add_reach(y, y)
    ones = jnp.ones((chans, 1), f32)

    upper_reach = lambda y: jnp.where(direct, reach[0, y], reach[1, y])
    lower_reach = lambda y: jnp.where(direct, reach[1, y], reach[0, y])
    emit_sides(
        lambda y, x: upper_reach(y) if x == layers - 1 else lower_reach(y),
        rows, 4, chans, depth, layers, ones, right, left,
    )


def from_rows(read, natural, spread):
    chans, layers, rows, _ = natural.shape
    for x in range(layers):

        def body(y, carry):
            row = read(y, x)
            for part in range(spread.shape[0]):
                spread[part, pl.ds(y, chans, stride=rows), :] = row[:, part * LANES : (part + 1) * LANES]
            return carry

        lax.fori_loop(0, rows, body, 0, unroll=4)
        for part in range(spread.shape[0]):
            natural[:, x, :, part * LANES : (part + 1) * LANES] = (
                spread[part].reshape(chans, rows, LANES).astype(bf16)
            )


def own_gradient_kernel(weights, field, total, natural, spread):
    chans, _, rows, _ = natural.shape
    total[...] = jnp.zeros(total.shape, f32)
    add_own(
        weights,
        (
            (field, 1, 0, 0, True),
            (field, 1, 1, 1, True),
            (field, rows - 2, 2, 2, False),
            (field, 1, rows, rows, True),
            (field, 1, rows + 1, rows + 1, True),
        ),
        total,
    )
    from_rows(lambda y, x: field[y + 1, x, :chans].astype(f32), natural, spread)


def update_kernel(partial, first, second, field, given, mask, natural, spread):
    chans, layers, _, _ = natural.shape
    direct, _, _ = place_flags()

    def value(y, x):
        gradient = partial[y, x * chans : (x + 1) * chans] - field[y + 1, x, :chans].astype(f32)
        if x == 0:
            gradient += jnp.where(direct, first[y], second[y]).astype(f32)
        if x == layers - 1:
            gradient += jnp.where(direct, second[y], first[y]).astype(f32)
        keep = 1.0 - mask[pl.ds(y, 1)].astype(f32)
        return given[y, x].astype(f32) - step_size * keep * gradient

    from_rows(value, natural, spread)


def call(kernel, shape, scratch, *args, reuse=None):
    return pl.pallas_call(
        kernel,
        out_shape=shape,
        in_specs=[IN_VMEM] * len(args),
        out_specs=jax.tree.map(lambda _: IN_VMEM, shape),
        input_output_aliases={} if reuse is None else {reuse: 0},
        scratch_shapes=scratch,
        compiler_params=pltpu.CompilerParams(vmem_limit_bytes=VMEM_LIMIT),
    )(*args)


def like(*shape, dtype=bf16):
    return jax.ShapeDtypeStruct(shape, dtype)


def around_x(layout, *segments):
    rows = sum(count for _, _, count in layout)
    layers, chans, depth = segments[0].shape[1:]
    side = like(rows, chans, depth)
    joined = pltpu.VMEM((rows, layers, chans, depth), bf16)
    kernel = functools.partial(sides_kernel, layout)
    right, left = call(kernel, (side, side), [joined], *segments)
    return send(right, to_right), send(left, to_left)


def step(kspace, kernel, mask):
    chans, layers, rows, depth = kspace.shape
    wide = layers * 2 * chans
    edge = outer_rows(rows)
    half = max(1, rows * MIDDLE // 32)
    count = rows - 2 * edge - 2 * half
    block = lambda size: like(size, layers, chans, depth)
    spread = pltpu.VMEM((depth // LANES, chans * rows, LANES), f32)
    total = like(rows + 2, wide, depth, dtype=f32)

    given, head, tail, outer, middle, inner = call(
        prepare_kernel,
        (block(rows), block(2), block(2), block(2 * edge), block(2 * half), block(count)),
        [spread, spread],
        kspace,
    )
    outer = send(outer, to_mirror)
    given_sides = around_x(((0, 0, rows),), given)
    middle = send(middle, to_mirror)
    top, bottom = send(tail, to_next), send(head, to_previous)

    early, early_sides, late, late_sides, adjoint, outward = call(
        weights_kernel,
        (
            like(3 * wide, 3 * layers * chans),
            like(2, 6 * chans, 3 * chans),
            like(3 * wide, 3 * layers * chans),
            like(2, 6 * chans, 3 * chans),
            like(3 * layers * chans, 3 * wide),
            like(2, 3 * chans, 6 * chans),
        ),
        [pltpu.VMEM((3, 3, 3, 2 * chans, 2 * chans), f32), pltpu.VMEM((3, 3, 3, chans, 2 * chans), f32)],
        kernel,
    )
    partial = call(early_kernel, total, [], early, given)
    virtual_top = send(outer[-2:], to_next)
    virtual_bottom = send(outer[:2], to_previous)
    inner = send(inner, to_mirror)
    layout = ((0, 0, 2), (1, 0, edge), (1, edge, edge), (2, 0, 2))
    outer_sides = around_x(layout, top, outer, bottom)
    partial = call(given_kernel, total, [], early_sides, *given_sides, partial, reuse=3)
    partial = call(
        outer_kernel, total, [],
        early, late, top, bottom, outer, partial, reuse=5,
    )

    middle_sides = around_x(((0, 0, 2 * half),), middle)
    partial = call(
        own_kernel, total, [], late, virtual_top, middle, virtual_bottom, partial, reuse=4
    )
    layout = ((0, 0, 2), (1, 0, count), (2, 0, 2))
    first, second = around_x(layout, virtual_top, inner, virtual_bottom)
    partial = call(
        inner_kernel, total, [],
        late, early_sides, late_sides, inner, *outer_sides, *middle_sides, partial, reuse=8,
    )
    side = like(rows, chans, depth)
    _, field, right, left = call(
        residual_kernel,
        (total, like(rows + 2, layers, 2 * chans, depth), side, side),
        [pltpu.VMEM((2, rows, chans, depth), f32)],
        late_sides, outward, first, second, partial,
        top, given, bottom, virtual_top, outer, middle, virtual_bottom, inner, reuse=4,
    )
    first, second = send(right, to_right), send(left, to_left)
    natural = like(chans, layers, rows, depth)
    partial, residual = call(
        own_gradient_kernel,
        (like(rows, layers * chans, depth, dtype=f32), natural),
        [spread],
        adjoint, field,
    )
    updated = call(update_kernel, natural, [spread], partial, first, second, field, given, mask)
    return updated, residual


def solution(mesh):
    spec = P(None, "kx", "ky", None)
    return jax.shard_map(
        step,
        mesh=mesh,
        in_specs=(spec, P(), P("ky", None)),
        out_specs=(spec, spec),
        check_vma=False,
    )
```

```python
import functools

import jax
import jax.numpy as jnp
from jax import lax
from jax.experimental import pallas as pl
from jax.experimental.pallas import tpu as pltpu
from jax.sharding import PartitionSpec as P


step_size = 0.5
LANES = 128
IN_VMEM = pl.BlockSpec(memory_space=pltpu.VMEM)
OUTER = 4
MIDDLE = 8
VMEM_LIMIT = 40 << 20
AXES = ("kx", "ky")
f32 = jnp.float32
bf16 = jnp.bfloat16


def on_line(a, b, nx, ny):
    inner = min(a, nx - 1 - a)
    return inner if b < ny // 2 else nx - 1 - inner


def line_device(a, b, nx, ny, place):
    near = b if b < ny // 2 else ny - 1 - b
    inner = min(place, nx - 1 - place)
    return (inner if a < nx // 2 else nx - 1 - inner), (near if place < nx // 2 else ny - 1 - near)


def to_mirror(a, b, nx, ny):
    return nx - 1 - a, ny - 1 - b


def to_right(a, b, nx, ny):
    place = on_line(a, b, nx, ny) + 1
    return line_device(a, b, nx, ny, place) if place < nx else None


def to_left(a, b, nx, ny):
    place = on_line(a, b, nx, ny) - 1
    return line_device(a, b, nx, ny, place) if place >= 0 else None


def to_next(a, b, nx, ny):
    return (a, b + 1) if b + 1 < ny else None


def to_previous(a, b, nx, ny):
    return (a, b - 1) if b > 0 else None


def send(value, move):
    nx, ny = lax.axis_size("kx"), lax.axis_size("ky")
    pairs = []
    for a in range(nx):
        for b in range(ny):
            target = move(a, b, nx, ny)
            if target is not None:
                pairs.append((a * ny + b, target[0] * ny + target[1]))
    return lax.ppermute(value, AXES, pairs)


def place_flags():
    a, b = lax.axis_index("kx"), lax.axis_index("ky")
    nx, ny = lax.axis_size("kx"), lax.axis_size("ky")
    near = b < ny // 2
    direct = near == (a < nx // 2)
    fold = (a == nx // 2) | (a == nx // 2 - 1)
    return direct, fold & jnp.logical_not(near), fold & near


def sign_rows(count, chans):
    row = lax.broadcasted_iota(jnp.int32, (count, 1), 0)
    return jnp.where(row % chans < chans // 2, 1.0, -1.0)


def dot(left, right):
    return jnp.dot(left, right, preferred_element_type=f32)


def reversal(depth):
    row = lax.broadcasted_iota(jnp.int32, (depth, depth), 0)
    col = lax.broadcasted_iota(jnp.int32, (depth, depth), 1)
    return jnp.where(row + col == depth - 1, 1.0, 0.0).astype(bf16)


def shifted(rows):
    depth = rows.shape[1]
    lane = lax.broadcasted_iota(jnp.int32, rows.shape, 1)
    before = jnp.where(lane == 0, 0, pltpu.roll(rows, 1, 1)).astype(rows.dtype)
    after = jnp.where(lane == depth - 1, 0, pltpu.roll(rows, depth - 1, 1)).astype(rows.dtype)
    return jnp.concatenate([before, rows, after], axis=0)


def flat(block):
    return block.reshape(-1, block.shape[-1])


def inside_y(y, count):
    b, ny = lax.axis_index("ky"), lax.axis_size("ky")
    return ((y > 0) | (b > 0)) & ((y < count - 1) | (b < ny - 1))


def weights_kernel(kernel, early, early_sides, late, late_sides, adjoint, outward, blocks, columns):
    chans = kernel.shape[3]
    wide = 2 * chans
    layers = early.shape[0] // (3 * wide)
    direct, fold_first, fold_second = place_flags()
    lane = lax.broadcasted_iota(jnp.int32, (wide, wide), 1)
    lane_sign = jnp.where(lane[:chans] % chans < chans // 2, 1.0, -1.0)
    signs = sign_rows(chans, chans) * lane_sign

    for dx in range(3):
        for dy in range(3):
            for dz in range(3):
                plain = kernel[dx, dy, dz].astype(f32)
                opposite = kernel[2 - dx, 2 - dy, 2 - dz].astype(f32)
                blocks[dx, dy, dz] = jnp.concatenate(
                    [plain, pltpu.roll(opposite * signs, chans, 1)], axis=0
                )
                column = jnp.concatenate([opposite, pltpu.roll(plain * signs, chans, 1)], axis=0)
                columns[dx, dy, dz] = jnp.transpose(column)[:chans]

    none = jnp.zeros((chans, wide), bf16)
    for dy in range(3):
        for x in range(layers):
            rows = pl.ds((dy * layers + x) * chans, chans)
            for dz in range(3):
                for source in range(layers):
                    dx = source - x + 1
                    start = (dz * layers + source) * wide
                    block = columns[dx, dy, dz].astype(bf16) if 0 <= dx < 3 else none
                    adjoint[rows, start : start + wide] = block
        for dz in range(3):
            rows, cols = pl.ds(dy * chans, chans), slice(dz * wide, (dz + 1) * wide)
            low, high = columns[0, dy, dz], columns[2, dy, dz]
            turn = lambda block: pltpu.roll(block, chans, 1) * lane_sign
            low_turned, high_turned = turn(columns[0, 2 - dy, 2 - dz]), turn(columns[2, 2 - dy, 2 - dz])
            right = jnp.where(direct, low, high)
            right = jnp.where(fold_second, jnp.where(direct, high_turned, low_turned), right)
            left = jnp.where(direct, high, low)
            left = jnp.where(fold_first, jnp.where(direct, low_turned, high_turned), left)
            outward[0, rows, cols] = right.astype(bf16)
            outward[1, rows, cols] = left.astype(bf16)

    half = lane < chans

    def pair(left, right, kind):
        left = jnp.where(kind, pltpu.roll(left, chans, 1), left)
        right = jnp.where(kind, right, pltpu.roll(right, chans, 1))
        return jnp.where(half, left, right).astype(bf16)

    empty = jnp.zeros((wide, wide), f32)
    for dy in range(3):
        for x in range(layers):
            rows = pl.ds((dy * layers + x) * wide, wide)
            for dz in range(3):
                get = lambda dx: blocks[dx, dy, dz] if 0 <= dx < 3 else empty
                start = dz * layers * chans
                for source in range(0, layers, 2):
                    ahead, behind = get(source - x + 1), get(source - x + 2)
                    cols = slice(start + source * chans, start + (source + 2) * chans)
                    early[rows, cols] = pair(ahead, behind, False)
                    late[rows, cols] = pair(ahead, behind, True)
        rows = pl.ds(dy * wide, wide)
        for slot, fold in ((0, fold_first), (1, fold_second)):
            lower = direct if slot == 0 else jnp.logical_not(direct)
            taps = [jnp.where(lower, blocks[0, dy, dz], blocks[2, dy, dz]) for dz in range(3)]
            for target, kind in ((early_sides, fold), (late_sides, jnp.logical_not(fold))):
                target[slot, rows, 0:wide] = pair(taps[0], taps[1], kind)
                target[slot, rows, wide : wide + chans] = pair(taps[2], taps[2], kind)[:, :chans]


def row_from(spread, y, chans, rows):
    return jnp.concatenate(
        [spread[part, pl.ds(y, chans, stride=rows), :] for part in range(spread.shape[0])], axis=1
    )


def prepare_kernel(
    natural, given, first_rows, last_rows, outer, middle, inner, spread, turned, staged, arrived
):
    chans, layers, rows, depth = natural.shape
    flip = reversal(depth)
    signs = sign_rows(chans, chans)
    groups, start = [], 0
    for ref in (outer, middle):
        groups.append((ref, start, ref.shape[0] // 2))
        start += ref.shape[0] // 2
    copies = [
        pltpu.make_async_copy(natural.at[:, x], staged.at[x], arrived.at[x]) for x in range(layers)
    ]
    for copy in copies:
        copy.start()
    for x in range(layers):
        copies[x].wait()
        whole = staged[x].reshape(chans * rows, depth)
        mirrored = dot(whole, flip)
        whole = whole.astype(f32)
        for part in range(spread.shape[0]):
            spread[part] = whole[:, part * LANES : (part + 1) * LANES]
            turned[part] = mirrored[:, part * LANES : (part + 1) * LANES]
        for y in range(rows):
            block = row_from(spread, y, chans, rows).astype(bf16)
            given[y, x] = block
            if y < 2:
                first_rows[y, x] = block
            if y >= rows - 2:
                last_rows[y - rows + 2, x] = block
            target = rows - 1 - y
            block = (row_from(turned, y, chans, rows) * signs).astype(bf16)
            for ref, start, half in groups:
                if start <= target < start + half:
                    ref[target - start, layers - 1 - x] = block
                if start <= rows - 1 - target < start + half:
                    ref[target - rows + start + 2 * half, layers - 1 - x] = block
            first_inner = (rows - inner.shape[0]) // 2
            if first_inner <= target < first_inner + inner.shape[0]:
                inner[target - first_inner, layers - 1 - x] = block


def emit_sides(read, rows, group, chans, depth, layers, signs, right, left):
    direct, fold_first, fold_second = place_flags()
    flip = reversal(depth)

    def write(target, upper, turned):
        def pick(y):
            return jnp.where(upper, read(y, layers - 1), read(y, 0))

        @pl.when(turned)
        def _():
            def body(j, carry):
                block = jnp.concatenate([pick(j * group + i).astype(bf16) for i in range(group)], axis=0)
                block = dot(block, flip)
                for i in range(group):
                    part = block[i * chans : (i + 1) * chans]
                    target[rows - 1 - j * group - i] = (part * signs).astype(bf16)
                return carry

            lax.fori_loop(0, rows // group, body, 0)

        @pl.when(jnp.logical_not(turned))
        def _():
            def body(y, carry):
                target[y] = pick(y).astype(bf16)
                return carry

            lax.fori_loop(0, rows, body, 0, unroll=2)

    write(right, direct, fold_second)
    write(left, jnp.logical_not(direct), fold_first)


def sides_kernel(layout, *refs):
    *segments, right, left, joined = refs
    rows, layers, chans, depth = joined.shape
    start = 0
    for index, offset, count in layout:
        joined[start : start + count] = segments[index][offset : offset + count]
        start += count
    signs = sign_rows(chans, chans)
    emit_sides(lambda y, x: joined[y, x], rows, 2 if rows % 4 else 4, chans, depth, layers, signs, right, left)


def add_part(total, part, place, columns):
    outs = part.shape[0] // 3
    for third in range(3):
        target = place - third
        if isinstance(target, int) and not 0 <= target < total.shape[0]:
            continue
        total[target, columns] = total[target, columns] + part[third * outs : (third + 1) * outs]


def add_rows(weights, read, count, place, total, columns, static):
    def one(y, place):
        add_part(total, dot(weights[...], shifted(flat(read(y)))), place, columns)

    if static:
        for y in range(count):
            one(y, place + y)
    else:

        def body(y, carry):
            one(y, place + y)
            return carry

        lax.fori_loop(0, count, body, 0, unroll=4)


def side_columns(total, layers):
    direct, _, _ = place_flags()
    wide = total.shape[1] // layers
    upper = (layers - 1) * wide
    first = pl.multiple_of(jnp.where(direct, 0, upper), wide)
    second = pl.multiple_of(jnp.where(direct, upper, 0), wide)
    return pl.ds(first, wide), pl.ds(second, wide)


def add_own(weights, segments, total):
    for ref, count, offset, place, static in segments:
        add_rows(
            weights, lambda y, ref=ref, offset=offset: ref[y + offset], count, place, total,
            slice(None), static,
        )


def add_sides(weights, first, second, offset, count, place, total, columns, static):
    def one(y, place):
        for slot, ref in ((0, first), (1, second)):
            part = dot(weights[slot], shifted(flat(ref[y + offset])))
            add_part(total, part, place, columns[slot])

    if static:
        for y in range(count):
            one(y, place + y)
    else:

        def body(y, carry):
            one(y, place + y)
            return carry

        lax.fori_loop(0, count, body, 0, unroll=4)


def early_kernel(weights, own, total):
    total[...] = jnp.zeros(total.shape, f32)
    add_own(weights, ((own, own.shape[0], 0, 2, False),), total)


def given_kernel(sides, first, second, partial, total):
    rows = total.shape[0] - 2
    layers = 3 * total.shape[1] // sides.shape[1]
    add_sides(sides, first, second, 0, rows, 2, total, side_columns(total, layers), False)


def outer_kernel(early, late, top, bottom, outer, partial, total):
    end, edge = total.shape[0], outer.shape[0] // 2
    add_own(early, ((top, 2, 0, 0, True), (bottom, 2, 0, end, True)), total)
    add_own(
        late,
        (
            (outer, edge, 0, 2, True),
            (outer, edge, edge, end - edge, True),
        ),
        total,
    )


def outer_rows(rows):
    return max(2, rows * OUTER // 32)


def own_kernel(late, virtual_top, middle, virtual_bottom, partial, total):
    end, half = total.shape[0], middle.shape[0] // 2
    edge = outer_rows(end - 2)
    add_own(
        late,
        (
            (virtual_top, 2, 0, 0, True),
            (middle, half, 0, 2 + edge, True),
            (middle, half, half, end - edge - half, True),
            (virtual_bottom, 2, 0, end, True),
        ),
        total,
    )


def inner_kernel(
    late, early_sides, late_sides, inner,
    first_outer, second_outer, first_middle, second_middle, partial, total,
):
    end, edge, half = total.shape[0], first_outer.shape[0] // 2 - 2, first_middle.shape[0] // 2
    add_own(late, ((inner, inner.shape[0], 0, 2 + edge + half, True),), total)
    columns = side_columns(total, 3 * total.shape[1] // early_sides.shape[1])
    for weights, first, second, offset, size, place in (
        (early_sides, first_outer, second_outer, 0, 2, 0),
        (late_sides, first_outer, second_outer, 2, edge, 2),
        (late_sides, first_outer, second_outer, 2 + edge, edge, end - edge),
        (early_sides, first_outer, second_outer, 2 + 2 * edge, 2, end),
        (late_sides, first_middle, second_middle, 0, half, 2 + edge),
        (late_sides, first_middle, second_middle, half, half, end - edge - half),
    ):
        add_sides(weights, first, second, offset, size, place, total, columns, True)


def residual_kernel(
    sides, outward, first, second, partial,
    top, given, bottom, virtual_top, virtual_outer, virtual_middle, virtual_bottom, virtual_inner,
    total, field, right, left, reach,
):
    rows, layers, chans, depth = given.shape
    span = rows + 2
    edge, half = virtual_outer.shape[0] // 2, virtual_middle.shape[0] // 2
    inner = rows - 2 * edge - 2 * half
    columns = side_columns(total, layers)
    for offset, count, place in ((0, 2, 0), (2, inner, 2 + edge + half), (2 + inner, 2, rows + 2)):
        add_sides(sides, first, second, offset, count, place, total, columns, True)

    def finish(target, k, t):
        both = jnp.concatenate([k, t], axis=1).astype(f32)
        value = total[target].reshape(layers, 2 * chans, depth) - both
        field[target] = jnp.where(inside_y(target, span), value, 0.0).astype(bf16)

    def loop(count, first_target, k, t):
        for y in range(count):
            finish(first_target + y, k(y), t(y))

    finish(0, top[1], virtual_top[1])
    y = 0
    for ref, offset, count in (
        (virtual_outer, 0, edge), (virtual_middle, 0, half), (virtual_inner, 0, inner),
        (virtual_middle, half, half), (virtual_outer, edge, edge),
    ):
        loop(
            count, 1 + y, lambda j, y=y: given[j + y],
            lambda j, ref=ref, offset=offset: ref[j + offset],
        )
        y += count
    finish(span - 1, bottom[0], virtual_bottom[0])

    direct, _, _ = place_flags()
    reach[...] = jnp.zeros(reach.shape, f32)

    def add_reach(y, place):
        upper, lower = field[y, layers - 1], field[y, 0]
        for slot, row in (
            (0, jnp.where(direct, upper, lower)), (1, jnp.where(direct, lower, upper))
        ):
            add_part(reach.at[slot], dot(outward[slot], shifted(row)), place, slice(None))

    def body(y, carry):
        add_reach(y, y)
        return carry

    for y in (0, 1):
        add_reach(y, y)
    lax.fori_loop(2, rows, body, 0, unroll=7 if (rows - 2) % 7 == 0 else 2)
    for y in (rows, rows + 1):
        add_reach(y, y)
    ones = jnp.ones((chans, 1), f32)

    upper_reach = lambda y: jnp.where(direct, reach[0, y], reach[1, y])
    lower_reach = lambda y: jnp.where(direct, reach[1, y], reach[0, y])
    emit_sides(
        lambda y, x: upper_reach(y) if x == layers - 1 else lower_reach(y),
        rows, 4, chans, depth, layers, ones, right, left,
    )


def from_rows(read, natural, spread):
    chans, layers, rows, _ = natural.shape
    for x in range(layers):

        def body(y, carry):
            row = read(y, x)
            for part in range(spread.shape[0]):
                spread[part, pl.ds(y, chans, stride=rows), :] = row[:, part * LANES : (part + 1) * LANES]
            return carry

        lax.fori_loop(0, rows, body, 0, unroll=4)
        for part in range(spread.shape[0]):
            natural[:, x, :, part * LANES : (part + 1) * LANES] = (
                spread[part].reshape(chans, rows, LANES).astype(bf16)
            )


def own_gradient_kernel(weights, field, given, mask, total, natural, spread):
    chans, layers, rows, _ = natural.shape
    total[...] = jnp.zeros(total.shape, f32)
    add_own(
        weights,
        (
            (field, 1, 0, 0, True),
            (field, 1, 1, 1, True),
            (field, rows - 2, 2, 2, False),
            (field, 1, rows, rows, True),
            (field, 1, rows + 1, rows + 1, True),
        ),
        total,
    )
    from_rows(lambda y, x: field[y + 1, x, :chans].astype(f32), natural, spread)

    def body(y, carry):
        keep = 1.0 - mask[pl.ds(y, 1)].astype(f32)
        for x in range(layers):
            part = slice(x * chans, (x + 1) * chans)
            gradient = total[y, part] - field[y + 1, x, :chans].astype(f32)
            total[y, part] = given[y, x].astype(f32) - step_size * keep * gradient
        return carry

    lax.fori_loop(0, rows, body, 0, unroll=2)


def update_kernel(partial, first, second, mask, natural, spread):
    chans, layers, _, _ = natural.shape
    direct, _, _ = place_flags()

    def value(y, x):
        value = partial[y, x * chans : (x + 1) * chans]
        keep = step_size * (1.0 - mask[pl.ds(y, 1)].astype(f32))
        if x == 0:
            value -= keep * jnp.where(direct, first[y], second[y]).astype(f32)
        if x == layers - 1:
            value -= keep * jnp.where(direct, second[y], first[y]).astype(f32)
        return value

    from_rows(value, natural, spread)


def call(kernel, shape, scratch, *args, reuse=None, space=pltpu.VMEM):
    return pl.pallas_call(
        kernel,
        out_shape=shape,
        in_specs=[pl.BlockSpec(memory_space=space)] * len(args),
        out_specs=jax.tree.map(lambda _: IN_VMEM, shape),
        input_output_aliases={} if reuse is None else {reuse: 0},
        scratch_shapes=scratch,
        compiler_params=pltpu.CompilerParams(vmem_limit_bytes=VMEM_LIMIT),
    )(*args)


def like(*shape, dtype=bf16):
    return jax.ShapeDtypeStruct(shape, dtype)


def around_x(layout, *segments):
    rows = sum(count for _, _, count in layout)
    layers, chans, depth = segments[0].shape[1:]
    side = like(rows, chans, depth)
    joined = pltpu.VMEM((rows, layers, chans, depth), bf16)
    kernel = functools.partial(sides_kernel, layout)
    right, left = call(kernel, (side, side), [joined], *segments)
    return send(right, to_right), send(left, to_left)


def step(kspace, kernel, mask):
    chans, layers, rows, depth = kspace.shape
    wide = layers * 2 * chans
    edge = outer_rows(rows)
    half = max(1, rows * MIDDLE // 32)
    count = rows - 2 * edge - 2 * half
    block = lambda size: like(size, layers, chans, depth)
    spread = pltpu.VMEM((depth // LANES, chans * rows, LANES), f32)
    total = like(rows + 2, wide, depth, dtype=f32)

    given, head, tail, outer, middle, inner = call(
        prepare_kernel,
        (block(rows), block(2), block(2), block(2 * edge), block(2 * half), block(count)),
        [
            spread,
            spread,
            pltpu.VMEM((layers, chans, rows, depth), bf16),
            pltpu.SemaphoreType.DMA((layers,)),
        ],
        kspace,
        space=pl.ANY,
    )
    outer = send(outer, to_mirror)
    given_sides = around_x(((0, 0, rows),), given)
    middle = send(middle, to_mirror)
    top, bottom = send(tail, to_next), send(head, to_previous)

    early, early_sides, late, late_sides, adjoint, outward = call(
        weights_kernel,
        (
            like(3 * wide, 3 * layers * chans),
            like(2, 6 * chans, 3 * chans),
            like(3 * wide, 3 * layers * chans),
            like(2, 6 * chans, 3 * chans),
            like(3 * layers * chans, 3 * wide),
            like(2, 3 * chans, 6 * chans),
        ),
        [pltpu.VMEM((3, 3, 3, 2 * chans, 2 * chans), f32), pltpu.VMEM((3, 3, 3, chans, 2 * chans), f32)],
        kernel,
    )
    partial = call(early_kernel, total, [], early, given)
    virtual_top = send(outer[-2:], to_next)
    virtual_bottom = send(outer[:2], to_previous)
    inner = send(inner, to_mirror)
    layout = ((0, 0, 2), (1, 0, edge), (1, edge, edge), (2, 0, 2))
    outer_sides = around_x(layout, top, outer, bottom)
    partial = call(given_kernel, total, [], early_sides, *given_sides, partial, reuse=3)
    partial = call(
        outer_kernel, total, [],
        early, late, top, bottom, outer, partial, reuse=5,
    )

    middle_sides = around_x(((0, 0, 2 * half),), middle)
    partial = call(
        own_kernel, total, [], late, virtual_top, middle, virtual_bottom, partial, reuse=4
    )
    layout = ((0, 0, 2), (1, 0, count), (2, 0, 2))
    first, second = around_x(layout, virtual_top, inner, virtual_bottom)
    partial = call(
        inner_kernel, total, [],
        late, early_sides, late_sides, inner, *outer_sides, *middle_sides, partial, reuse=8,
    )
    side = like(rows, chans, depth)
    _, field, right, left = call(
        residual_kernel,
        (total, like(rows + 2, layers, 2 * chans, depth), side, side),
        [pltpu.VMEM((2, rows, chans, depth), f32)],
        late_sides, outward, first, second, partial,
        top, given, bottom, virtual_top, outer, middle, virtual_bottom, inner, reuse=4,
    )
    first, second = send(right, to_right), send(left, to_left)
    natural = like(chans, layers, rows, depth)
    partial, residual = call(
        own_gradient_kernel,
        (like(rows, layers * chans, depth, dtype=f32), natural),
        [spread],
        adjoint, field, given, mask,
    )
    updated = call(update_kernel, natural, [spread], partial, first, second, mask)
    return updated, residual


def solution(mesh):
    spec = P(None, "kx", "ky", None)
    return jax.shard_map(
        step,
        mesh=mesh,
        in_specs=(spec, P(), P("ky", None)),
        out_specs=(spec, spec),
        check_vma=False,
    )
```
